32 devices in a mesh: frame: 16 (over z, y, x), row: 2 (over core).
Axes of the slice: x: 2, y: 2, z: 4, core: 2. Of those that a mesh axis runs over, the one named last changes fastest.
Arguments:
- latents: bfloat16 [32, 16, 36, 320], P('frame', 'row'), may hold values from -6 to 6
- conv_first: bfloat16 [3, 3, 320, 320], replicated, may hold values from -0.109375 to 0.109375
- conv_second: bfloat16 [3, 3, 320, 320], replicated, may hold values from -0.109375 to 0.109375
- conv_time: bfloat16 [3, 320, 320], replicated, may hold values from -0.1875 to 0.1875
- cond_start: float32 [320], replicated, may hold values from -4 to 4
- cond_end: float32 [320], replicated, may hold values from -4 to 4
Outputs:
- blended: bfloat16 [32, 16, 36, 320], P('frame', 'row')
The draws below stay inside these ranges and needn't reach their ends.
All inputs are finite; a program needn't handle non-finite values.
Results may differ from the reference program's by a relative error of at most 0.0047.
Values may be sent and summed in bfloat16 or wider, within the bound.
No kernel may reach another device: no remote copies, remote signals or barrier semaphores. Data moves between devices by JAX's collectives and lax.ppermute only.
A program may use at most 64 MiB of HBM per device.

```python
import jax
import jax.numpy as jnp

C = 320
COLS = 36
FRAMES = 32
ROWS = 16


def levels(key, extent, pieces, smallest, high):
    loudness, own = 1.0, jax.random.fold_in(key, 6)
    for dim, shards_of in pieces:
        heights = jnp.exp(jax.random.uniform(jax.random.fold_in(own, dim), (shards_of,), jnp.float32, smallest / len(pieces), high / len(pieces)))
        loudness = loudness * jnp.repeat(heights, extent[dim] // shards_of).reshape([-1 if axis == dim else 1 for axis in range(len(extent))])
    return loudness


def gaussian(stream_key, extent, spread, bound, split=(), dtype=jnp.bfloat16):
    array = spread * jax.random.normal(stream_key, extent, jnp.float32)
    if split:
        array = array * levels(stream_key, extent, split, -0.22, 0.18)
    return jnp.clip(array, -bound, bound).astype(dtype)


def setup_inputs(seed: int = 0) -> dict:
    seeds = jax.random.split(jax.random.key(seed), 7)
    return {
        "latents": gaussian(seeds[0], (FRAMES, ROWS, COLS, C), 1.0, 6.0, ((0, 16), (1, 2))),
        "conv_first": gaussian(seeds[1], (3, 3, C, C), (9 * C) ** -0.5, 0.109375),
        "conv_second": gaussian(seeds[2], (3, 3, C, C), (9 * C) ** -0.5, 0.109375),
        "conv_time": gaussian(seeds[3], (3, C, C), (3 * C) ** -0.5, 0.1875),
        "cond_start": gaussian(seeds[4], (C,), 1.0, 4.0, (), jnp.float32),
        "cond_end": gaussian(seeds[5], (C,), 1.0, 4.0, (), jnp.float32),
    }


def spatial(video, weight):
    padded = jnp.pad(video, ((0, 0), (1, 1), (1, 1), (0, 0)))
    rows_n = video.shape[1]
    cols_n = video.shape[2]
    total = jnp.zeros(video.shape[:3] + (weight.shape[3],), jnp.float32)
    for a in range(3):
        for b in range(3):
            window = padded[:, a:a + rows_n, b:b + cols_n, :].astype(jnp.float32)
            total = total + jnp.einsum("frwc,cd->frwd", window, weight[a, b].astype(jnp.float32))
    return total


def temporal(resid, weight):
    padded = jnp.pad(resid, ((1, 1), (0, 0), (0, 0), (0, 0))).astype(jnp.float32)
    wide = weight.astype(jnp.float32)
    total = jnp.einsum("frwc,cd->frwd", padded[:-2], wide[0])
    total = total + jnp.einsum("frwc,cd->frwd", padded[1:-1], wide[1])
    total = total + jnp.einsum("frwc,cd->frwd", padded[2:], wide[2])
    return total


def one_pass(video, conv_first, conv_second, conv_time, cond):
    hidden = jax.nn.silu(spatial(video, conv_first) + cond).astype(jnp.bfloat16)
    resid = (video.astype(jnp.float32) + spatial(hidden, conv_second)).astype(jnp.bfloat16)
    mixed = temporal(resid, conv_time)
    return resid.astype(jnp.float32) + jax.nn.silu(mixed)


def reference(latents, conv_first, conv_second, conv_time, cond_start, cond_end):
    forward = one_pass(latents, conv_first, conv_second, conv_time, cond_start)
    backward = one_pass(jnp.flip(latents, 0), conv_first, conv_second, conv_time, cond_end)
    return (0.5 * (forward + jnp.flip(backward, 0))).astype(jnp.bfloat16)
```

```python
import functools

import jax
import jax.numpy as jnp
from jax import lax
from jax.experimental import pallas as pl
from jax.experimental.pallas import tpu as pltpu
from jax.sharding import PartitionSpec as P

F32 = jnp.float32
BF16 = jnp.bfloat16
LANES = 128
SUB = 8
CHUNK = 2

NEAR, FAR, TAP_FAR, TAP_NEAR, HAS_FAR, HAS_UP, HAS_DOWN = range(7)


def silu(u):
    return 0.5 * u * (1.0 + jnp.tanh(0.5 * u))


def split(value, main):
    tail = value[..., main:]
    return value[..., :main], jnp.concatenate([tail, jnp.zeros_like(tail)], axis=-1)


def rows_of(shape):
    return lax.broadcasted_iota(jnp.int32, shape, len(shape) - 2)


def turn(value, shift):
    shift %= value.shape[-2]
    return value if shift == 0 else pltpu.roll(value, shift, value.ndim - 2)


def beside(low, high):
    return low + pltpu.roll(high, LANES // 2, high.ndim - 1)


def half_tile(value, which):
    lane = lax.broadcasted_iota(jnp.int32, value.shape, value.ndim - 1)
    if which:
        value = pltpu.roll(value, LANES // 2, value.ndim - 1)
    return jnp.where(lane < LANES // 2, value, 0.0)


def pack(low, high):
    (low_main, low_tail), (high_main, high_tail) = low, high
    return jnp.concatenate([low_main, high_main, beside(low_tail, high_tail)], axis=-1)


def unpack(value, main, which):
    return value[..., which * main : (which + 1) * main], half_tile(value[..., 2 * main :], which)


def edge_rows(first, second):
    row = rows_of(first.shape)
    return jnp.where(
        row < 2, first, jnp.where(row < 4, turn(first, 4), jnp.where(row < 6, turn(second, 4), second))
    )


class Stencil:
    def __init__(self, here, later, main):
        self.here, self.later, self.main = here, later, main
        self.held = None
        self.at = 0

    def add(self, prev, mid, nxt, first=None):
        pieces = [prev[0], mid[0], nxt[0], beside(prev[1], mid[1]), nxt[1]]
        if self.held is None:
            self.held = [jnp.zeros_like(p[:1]) for p in pieces] if first is None else first
        lane, start = 0, self.at * SUB
        for i, piece in enumerate(pieces):
            size, width = piece.shape[0] * SUB, piece.shape[-1]
            self.here[start : start + size, lane : lane + width] = piece.reshape(size, width).astype(BF16)
            moved = jnp.concatenate([self.held[i], piece[:-1]], axis=0)
            self.later[start : start + size, lane : lane + width] = moved.reshape(size, width).astype(BF16)
            self.held[i] = piece[-1:]
            lane += width
        self.at += pieces[0].shape[0]

    def close(self, last=None):
        lane, start = 0, self.at * SUB
        for i, held in enumerate(self.held):
            width = held.shape[-1]
            after = jnp.zeros_like(held) if last is None else last[i]
            moved = jnp.concatenate([held, after], axis=0)
            self.later[start : start + 2 * SUB, lane : lane + width] = moved.reshape(2 * SUB, width).astype(BF16)
            lane += width
        self.size = start

    def conv(self, weight):
        size, main = self.size, self.main

        def taps(column):
            parts = [weight[a, column, :main] for a in range(3)] + [weight[a, column, main:] for a in range(3)]
            return jnp.concatenate(parts + [jnp.zeros_like(parts[-1])], axis=0)

        total = jnp.dot(self.here[:size], taps(1), preferred_element_type=F32)
        total += jnp.dot(self.later[:size], taps(0), preferred_element_type=F32)
        total += jnp.dot(self.later[2 * SUB : 2 * SUB + size], taps(2), preferred_element_type=F32)
        return total


def columns(ref, start, main, size=CHUNK):
    return split(ref[start : start + size].astype(F32), main)


def conv_main(cols, main, source, weight, here, later):
    stencil = Stencil(here, later, main)
    for c in range(0, cols, CHUNK):
        mid = source(c)
        stencil.add([turn(p, 1) for p in mid], mid, [turn(p, -1) for p in mid])
    stencil.close()
    return stencil.conv(weight)


def edge_stencil(flags, own, up, down, main, here, later):
    stencil = Stencil(here, later, main)
    count = own.shape[0]

    def one(start, size):
        middle = columns(own, start, main, size)
        above = [jnp.where(flags[HAS_UP] > 0, p, 0.0) for p in columns(up, start, main, size)]
        below = [jnp.where(flags[HAS_DOWN] > 0, p, 0.0) for p in columns(down, start, main, size)]
        prev, mid, nxt = [], [], []
        for m, a, b in zip(middle, above, below):
            j = lax.rem(rows_of(m.shape), 4)
            prev.append(jnp.where(j < 2, turn(a, -2), m))
            mid.append(
                jnp.where(j < 1, turn(a, -3), jnp.where(j < 2, turn(m, 1), jnp.where(j < 3, turn(m, -1), turn(b, 3))))
            )
            nxt.append(jnp.where(j < 2, m, turn(b, 2)))
        return prev, mid, nxt

    return stencil, one, count


def edge_hidden(flags, total, cond, main):
    u = total + cond
    j = lax.rem(rows_of(u.shape), 4)
    h = silu(u)
    h = jnp.where((j > 0) | (flags[HAS_UP] > 0), h, 0.0)
    return jnp.where((j < 3) | (flags[HAS_DOWN] > 0), h, 0.0)


def second_conv(cols, main, spread, edges, cond, weight, here, later):
    stencil = Stencil(here, later, main)
    for c in range(0, cols, CHUNK):
        u = spread[c * SUB : (c + CHUNK) * SUB] + cond
        h = split(silu(u).reshape(CHUNK, SUB, u.shape[-1]), main)
        edge, base = edges(c)
        prev, mid, nxt = [], [], []
        for v, e in zip(h, edge):
            row = rows_of(v.shape)
            v = jnp.where(row == 0, turn(e, -(base + 1)), jnp.where(row == 7, turn(e, 7 - (base + 2)), v))
            mid.append(v)
            prev.append(jnp.where(row == 0, turn(e, -base), turn(v, 1)))
            nxt.append(jnp.where(row == 7, turn(e, 7 - (base + 3)), turn(v, -1)))
        stencil.add(prev, mid, nxt)
    stencil.close()
    return stencil.conv(weight)


def prepare_kernel(main, flags, video, edge, sent):
    cols = video.shape[1]
    near, far = flags[NEAR], flags[FAR]
    half = cols // 2
    for c in range(0, half, CHUNK):
        low = split(video[far, c : c + CHUNK].astype(F32), main)
        high = split(video[far, half + c : half + c + CHUNK].astype(F32), main)
        sent[c : c + CHUNK] = pack(low, high).astype(BF16)
    for c in range(0, cols, CHUNK):
        edge[c : c + CHUNK] = edge_rows(video[near, c : c + CHUNK].astype(F32), video[far, c : c + CHUNK].astype(F32)).astype(BF16)


def own_kernel(main, flags, video, weight, spread, here, later):
    cols = video.shape[1]
    for i, which in enumerate((NEAR, FAR)):
        f = flags[which]
        spread[i] = conv_main(
            cols, main, lambda c: split(video[f, c : c + CHUNK].astype(F32), main), weight, here.at[i], later.at[i]
        )


def residual(cols, main, source, spread, edges, conds, second, here, later, write):
    for p in range(2):
        added = second_conv(cols, main, spread, functools.partial(edges, p), conds[p], second, here.at[p], later.at[p])
        write(p, source, added)


def edge_kernel(main, flags, video, own, up, down, spread, cond, first, second, edge_h, r, sent, here, later):
    cols = video.shape[1]
    stencil, one, count = edge_stencil(flags, own, up, down, main, here.at[0], later.at[0])
    for c in range(0, count, CHUNK):
        stencil.add(*one(c, CHUNK))
    stencil.close()
    total = stencil.conv(first)
    total = total.reshape(count, SUB, total.shape[-1])
    for p in range(2):
        edge_h[p] = edge_hidden(flags, total, cond[p : p + 1], main)
    near = flags[NEAR]
    for p in range(2):
        added = second_conv(
            cols, main, spread.at[0], lambda c: (split(edge_h[p, c : c + CHUNK], main), 0), cond[p : p + 1], second,
            here.at[p], later.at[p],
        )
        r[p] = (video[near].astype(F32).reshape(added.shape) + added).astype(BF16)
    size = CHUNK * SUB
    for s in range(0, cols * SUB, size):
        low, high = (split(r[p, s : s + size].astype(F32), main) for p in range(2))
        sent[s : s + size] = pack(low, high).astype(BF16)


def relay_kernel(main, got, edge):
    half = got.shape[0]
    for c in range(0, half, CHUNK):
        value = got[c : c + CHUNK].astype(F32)
        low, high = unpack(value, main, 0), unpack(value, main, 1)
        tail = edge.shape[-1] - main
        edge[c : c + CHUNK, :, :main] = edge_rows(low[0], high[0]).astype(BF16)
        edge[c : c + CHUNK, :, main:] = edge_rows(low[1], high[1])[..., :tail].astype(BF16)


def other_kernel(main, flags, video, spread, edge_h, cond, second, got, first, r, far_spread, here, later):
    cols = video.shape[1]
    far = flags[FAR]
    for p in range(2):
        added = second_conv(
            cols, main, spread.at[1], lambda c: (split(edge_h[p, c : c + CHUNK], main), 4), cond[p : p + 1], second,
            here.at[p], later.at[p],
        )
        r[p] = (video[far].astype(F32).reshape(added.shape) + added).astype(BF16)
    half = cols // 2
    far_spread[...] = conv_main(
        cols, main, lambda c: unpack(got[c % half : c % half + CHUNK].astype(F32), main, c // half), first,
        here.at[0], later.at[0],
    )


def far_kernel(main, flags, got, own, up, down, spread, cond, first, second, r_near, r_far, taps, out, mixed, edge_h, r, here, later):
    half = got.shape[0]
    cols = 2 * half
    stencil, one, count = edge_stencil(flags, own, up, down, main, here.at[0], later.at[0])

    def pieces(column):
        prev, mid, nxt = one(column, 1)
        return [prev[0], mid[0], nxt[0], beside(prev[1], mid[1]), nxt[1]]

    before = [jnp.where(rows_of(p.shape) < 4, 0.0, turn(p, 4)) for p in pieces(count - 1)]
    after = [jnp.where(rows_of(p.shape) < 4, turn(p, 4), 0.0) for p in pieces(0)]
    for c in range(0, count, CHUNK):
        stencil.add(*one(c, CHUNK), first=before)
    stencil.close(after)
    total = stencil.conv(first)
    total = total.reshape(count, SUB, total.shape[-1])
    for p in range(2):
        edge_h[p] = edge_hidden(flags, total, cond[p : p + 1], main)
    size = CHUNK * SUB
    for p in range(2):
        added = second_conv(
            cols, main, spread, lambda c: (split(edge_h[p, c % half : c % half + CHUNK], main), c // half * 4),
            cond[p : p + 1], second, here.at[p], later.at[p],
        )
        for c in range(0, cols, CHUNK):
            x = unpack(got[c % half : c % half + CHUNK].astype(F32), main, c // half)
            s = c * SUB
            for x_part, at in zip(x, (slice(0, main), slice(main, added.shape[-1]))):
                part = added[s : s + size, at]
                x_part = x_part.reshape(size, x_part.shape[-1])[:, : part.shape[-1]]
                r[p, s : s + size, at] = jnp.where(flags[HAS_FAR] > 0, x_part + part, 0.0).astype(BF16)
    to_far, to_near = taps[flags[TAP_FAR]], taps[flags[TAP_NEAR]]
    blend = None
    for p in range(2):
        earlier, later_tap = (to_far, to_near) if p == 0 else (to_near, to_far)
        t = jnp.dot(r[p], earlier, preferred_element_type=F32)
        t += jnp.dot(r_far[p], taps[1], preferred_element_type=F32)
        t += jnp.dot(r_near[p], later_tap, preferred_element_type=F32)
        t = r_far[p].astype(F32) + silu(t)
        blend = t if blend is None else blend + t
        mixed[p] = jnp.dot(r_far[p], earlier, preferred_element_type=F32) + jnp.dot(
            r_near[p], taps[1], preferred_element_type=F32
        )
    out[...] = (0.5 * blend).astype(BF16)


def last_kernel(main, flags, got, mixed, r_near, taps, done, out, staged, sems):
    tail = r_near.shape[-1] - main
    first = pltpu.make_async_copy(done, out.at[flags[FAR]], sems.at[0])
    first.start()
    to_far, to_near = taps[flags[TAP_FAR]], taps[flags[TAP_NEAR]]
    blend = None
    for p in range(2):
        tap = to_near if p == 0 else to_far
        tail_value = half_tile(got[:, 2 * main :].astype(F32), p).astype(BF16)
        t = mixed[p] + jnp.dot(got[:, p * main : (p + 1) * main], tap[:main], preferred_element_type=F32)
        t += jnp.dot(tail_value[:, :tail], tap[main:], preferred_element_type=F32)
        t = r_near[p].astype(F32) + silu(t)
        blend = t if blend is None else blend + t
    staged[...] = (0.5 * blend).astype(BF16).reshape(staged.shape)
    second = pltpu.make_async_copy(staged, out.at[flags[NEAR]], sems.at[1])
    second.start()
    first.wait()
    second.wait()


VMEM = pl.BlockSpec(memory_space=pltpu.VMEM)
SMEM = pl.BlockSpec(memory_space=pltpu.SMEM)
ANY = pl.BlockSpec(memory_space=pl.ANY)


def call(kernel, outs, args, scratch=(), name=None, flops=0, out_specs=None, limit=20):
    return pl.pallas_call(
        kernel,
        out_shape=outs,
        in_specs=[SMEM if a.dtype == jnp.int32 else VMEM for a in args],
        out_specs=out_specs or jax.tree.map(lambda _: VMEM, outs),
        scratch_shapes=list(scratch),
        name=name,
        cost_estimate=pl.CostEstimate(flops=flops, bytes_accessed=1 << 20, transcendentals=0),
        compiler_params=pltpu.CompilerParams(vmem_limit_bytes=limit << 20),
    )(*args)


def pairs(count, start):
    links = [(i, i + 1) for i in range(start, count - 1, 2)]
    return links + [(b, a) for a, b in links]


def row_neighbours(edge):
    count = lax.axis_size("row")
    if count == 1:
        return edge, edge
    first = lax.ppermute(edge, "row", pairs(count, 0))
    if count == 2:
        return first, first
    second = lax.ppermute(edge, "row", pairs(count, 1))
    even = lax.axis_index("row") % 2 == 0
    return jnp.where(even, second, first), jnp.where(even, first, second)


def shards(latents, conv_first, conv_second, conv_time, cond_start, cond_end):
    _, rows, cols, channels = latents.shape
    main = channels // LANES * LANES
    assert latents.shape[0] == 2 and rows == SUB and 2 * (channels - main) == LANES and cols % (2 * CHUNK) == 0
    pixels = rows * cols
    width = 3 * main + 2 * LANES
    frames_n, rows_n = lax.axis_size("frame"), lax.axis_size("row")
    frame, row = lax.axis_index("frame"), lax.axis_index("row")
    odd = frame % 2
    has_far = jnp.where(odd == 1, frame < frames_n - 1, frame > 0)
    flags = jnp.stack([1 - odd, odd, 2 * odd, 2 - 2 * odd, has_far, row > 0, row < rows_n - 1]).astype(jnp.int32)

    video = jnp.transpose(latents, (0, 2, 1, 3))
    cond = jnp.stack([cond_start, cond_end])
    taps = channels * channels * 2

    def struct(*shape, dtype=BF16):
        return jax.ShapeDtypeStruct(shape, dtype)

    stencils = [pltpu.VMEM((2, pixels, width), BF16), pltpu.VMEM((2, pixels + 2 * SUB, width), BF16)]
    edge, sent = call(
        functools.partial(prepare_kernel, main),
        (struct(cols, SUB, channels), struct(cols // 2, SUB, 2 * main + LANES)),
        (flags, video), name="prepare",
    )
    got_far = lax.ppermute(sent, "frame", pairs(frames_n, 1))
    up, down = row_neighbours(edge)
    spread = call(
        functools.partial(own_kernel, main), struct(2, pixels, channels, dtype=F32), (flags, video, conv_first),
        stencils, "own", 18 * pixels * taps,
    )
    edge_h, r_near, sent_near = call(
        functools.partial(edge_kernel, main),
        (struct(2, cols, SUB, channels, dtype=F32), struct(2, pixels, channels), struct(pixels, 2 * main + LANES)),
        (flags, video, edge, up, down, spread, cond, conv_first, conv_second), stencils, "near", 27 * pixels * taps,
    )
    got_near = lax.ppermute(sent_near, "frame", pairs(frames_n, 0))
    far_edge = call(functools.partial(relay_kernel, main), struct(cols // 2, SUB, channels), (got_far,), name="relay")
    far_up, far_down = row_neighbours(far_edge)
    r_far, far_spread = call(
        functools.partial(other_kernel, main), (struct(2, pixels, channels), struct(pixels, channels, dtype=F32)),
        (flags, video, spread, edge_h, cond, conv_second, got_far, conv_first), stencils, "other", 27 * pixels * taps,
    )
    done, mixed = call(
        functools.partial(far_kernel, main), (struct(pixels, channels), struct(2, pixels, channels, dtype=F32)),
        (flags, got_far, far_edge, far_up, far_down, far_spread, cond, conv_first, conv_second, r_near, r_far, conv_time),
        [pltpu.VMEM((2, cols // 2, SUB, channels), F32), pltpu.VMEM((2, pixels, channels), BF16), *stencils],
        "far", 33 * pixels * taps,
    )
    out = call(
        functools.partial(last_kernel, main), struct(2, cols, SUB, channels),
        (flags, got_near, mixed, r_near, conv_time, done.reshape(cols, SUB, channels)),
        [pltpu.VMEM((cols, SUB, channels), BF16), pltpu.SemaphoreType.DMA((2,))], "last", 2 * pixels * taps, ANY,
    )
    return jnp.transpose(out, (0, 2, 1, 3))


def solution(mesh):
    placed = (P("frame", "row", None, None), P(), P(), P(), P(), P())
    return jax.shard_map(
        shards, mesh=mesh, in_specs=placed, out_specs=P("frame", "row", None, None), check_vma=False
    )
```

```python
import functools

import jax
import jax.numpy as jnp
from jax import lax
from jax.experimental import pallas as pl
from jax.experimental.pallas import tpu as pltpu
from jax.sharding import PartitionSpec as P

F32 = jnp.float32
BF16 = jnp.bfloat16
LANES = 128
HALF = LANES // 2
SUB = 8
CHUNK = 2
PAD = 2 * SUB

NEAR, FAR, TAP_FAR, TAP_NEAR, HAS_FAR, HAS_UP, HAS_DOWN = range(7)


def split(value, main):
    tail = value[..., main:]
    if tail.shape[-1] < LANES:
        tail = jnp.concatenate([tail, jnp.zeros_like(tail)], axis=-1)
    return [value[..., :main], tail]


def rows_of(value):
    return lax.broadcasted_iota(jnp.int32, value.shape, value.ndim - 2)


def lanes_of(value):
    return lax.broadcasted_iota(jnp.int32, value.shape, value.ndim - 1)


def turn(value, shift):
    shift %= value.shape[-2]
    return value if shift == 0 else pltpu.roll(value, shift, value.ndim - 2)


def swap_halves(value):
    return pltpu.roll(value, HALF, value.ndim - 1)


def beside(low, high):
    return jnp.where(lanes_of(low) < HALF, low, swap_halves(high))


def unpack(value, main, which):
    tail = value[..., 2 * main :]
    return [value[..., which * main : (which + 1) * main], swap_halves(tail) if which else tail]


def store(ref, start, value):
    main, tail = value
    width = main.shape[-1]
    ref[pl.ds(start, main.shape[0]), :, :width] = main.astype(ref.dtype)
    ref[pl.ds(start, main.shape[0]), :, width:] = tail[..., : ref.shape[-1] - width].astype(ref.dtype)


def edges_of(column, count):
    def tile(g):
        outer, second = None, None
        for j in range(4):
            x = column(j * count + g)
            z = [jnp.where(rows_of(v) == 7, turn(v, 1), turn(v, -1)) for v in x]
            x, z = [turn(v, 2 * j) for v in x], [turn(v, 2 * j) for v in z]
            if j == 0:
                outer, second = x, z
            else:
                at = lambda v: (rows_of(v) == (2 * j + 7) % 8) | (rows_of(v) == 2 * j)
                outer = [jnp.where(at(v), v, o) for v, o in zip(x, outer)]
                second = [jnp.where(at(v), v, o) for v, o in zip(z, second)]
        return outer, second

    return tile


class Stencil:
    def __init__(self, here, start=0):
        self.here = here
        self.row = start

    @staticmethod
    def pieces(prev, mid, nxt):
        return [prev[0], mid[0], nxt[0], beside(prev[1], mid[1]), nxt[1]]

    def put(self, pieces):
        size, lane = pieces[0].shape[0] * SUB, 0
        for piece in pieces:
            width = piece.shape[-1]
            self.here[self.row : self.row + size, lane : lane + width] = piece.reshape(size, width).astype(BF16)
            lane += width
        self.row += size


def pack_tails(weight, tails, main):
    row = 0
    for part in (slice(0, main), slice(main, None)):
        for a in range(3):
            left, mid, right = (weight[a, b, part, main:] for b in range(3))
            size = left.shape[0]
            tails[row : row + size, :LANES] = jnp.concatenate([left, mid], axis=1)
            tails[row : row + size, LANES:] = jnp.concatenate([right, jnp.zeros_like(right)], axis=1)
            row += size
    tails[row:] = jnp.zeros_like(tails[row:])


def convolve(here, weight, tails, total, start, size, main, into=0):
    def taps(column):
        parts = [weight[a, column, :main, :main] for a in range(3)] + [weight[a, column, main:, :main] for a in range(3)]
        return jnp.concatenate(parts + [jnp.zeros_like(parts[-1])], axis=0)

    def left(by):
        first = start + by * SUB
        return here[first : first + size]

    rows = slice(into, into + size)
    out = jnp.dot(left(1), taps(1), preferred_element_type=F32)
    out += jnp.dot(left(0), taps(0), preferred_element_type=F32)
    out += jnp.dot(left(2), taps(2), preferred_element_type=F32)
    total[rows, :main] = out
    total[rows, main:] = jnp.dot(left(1), tails[...], preferred_element_type=F32)


def tail_of(left, mid, right):
    return left[..., :LANES] + swap_halves(mid[..., :LANES]) + right[..., LANES:]


def frame_sum(total, c, cols, main, base=0):
    out, tail = [], []
    for i in range(c, c + CHUNK):
        s = base + i * SUB
        mid = total[s : s + SUB, main:]
        left = total[s - SUB : s, main:] if i > 0 else jnp.zeros_like(mid)
        right = total[s + SUB : s + 2 * SUB, main:] if i < cols - 1 else jnp.zeros_like(mid)
        out.append(total[s : s + SUB, :main])
        tail.append(tail_of(left, mid, right))
    return [jnp.stack(out), jnp.stack(tail)]


def edge_sum(total, g, count, main, base):
    mid = total[base + g * SUB : base + (g + 1) * SUB, main:]
    row = rows_of(mid)
    if g > 0:
        left = total[base + (g - 1) * SUB : base + g * SUB, main:]
    else:
        left = jnp.where((row == 7) | (row == 0), 0.0, turn(total[base + (count - 1) * SUB : base + count * SUB, main:], 2))
    if g < count - 1:
        right = total[base + (g + 1) * SUB : base + (g + 2) * SUB, main:]
    else:
        right = jnp.where((row == 5) | (row == 6), 0.0, turn(total[base : base + SUB, main:], -2))
    return [total[base + g * SUB : base + (g + 1) * SUB, :main], tail_of(left, mid, right)]


def edge_stencil(flags, outer, up, down, count, main, here, start):
    nearby = []
    has_up, has_down = flags[HAS_UP] > 0, flags[HAS_DOWN] > 0

    def pieces(g):
        prev, mid, nxt = [], [], []
        ups, downs = [up(k, g) for k in range(2)], [down(k, g) for k in range(2)]
        own = outer(g)
        for i in range(2):
            above = lax.rem(rows_of(own[i]), 2) == 1
            crossed = jnp.where(above, turn(own[i], -1), turn(own[i], 1))
            u_out, u_sec = (jnp.where(has_up, ups[k][i], 0.0) for k in range(2))
            d_out, d_sec = (jnp.where(has_down, downs[k][i], 0.0) for k in range(2))
            prev.append(jnp.where(above, u_sec, crossed))
            mid.append(jnp.where(above, u_out, d_out))
            nxt.append(jnp.where(above, crossed, d_sec))
        nearby.append(mid)
        return [p[None] for p in Stencil.pieces(prev, mid, nxt)]

    def wrap(values, shift, first, last):
        return [jnp.where((rows_of(v) == first) | (rows_of(v) == last), 0.0, turn(v, shift)) for v in values]

    tiles = [pieces(g) for g in range(count)]
    before, after = wrap(tiles[-1], 2, 7, 0), wrap(tiles[0], -2, 5, 6)
    tiles = [before, *tiles, after]
    stencil = Stencil(here, start)
    for tile in tiles:
        stencil.put(tile)
    return nearby


def inner_stencil(column, edge, cols, count, here, start=0):
    stencil = Stencil(here, start)
    blank = None
    for c in range(0, cols, CHUNK):
        mid = column(c)
        outer = [[turn(v, -2 * (i // count)) for v in edge(i % count)] for i in range(c, c + CHUNK)]
        prev, nxt = [], []
        for k, v in enumerate(mid):
            e = jnp.stack([o[k] for o in outer])
            prev.append(turn(jnp.where(rows_of(v) == 7, e, v), 1))
            nxt.append(turn(jnp.where(rows_of(v) == 0, e, v), -1))
        pieces = Stencil.pieces(prev, mid, nxt)
        if blank is None:
            blank = [jnp.zeros_like(p[:1]) for p in pieces]
            stencil.put(blank)
        stencil.put(pieces)
    stencil.put(blank)


def half_silu(y):
    return y + y * jnp.tanh(y)


def stage(flags):
    return pl.when(flags[NEAR] >= 0)


def cond_halves(cond, main):
    return [0.5 * v for v in split(cond[...].reshape(1, cond.shape[-1]), main)]


def spread_halves(total, spread, cols, count, main, base, edge_base):
    for c in range(0, cols, CHUNK):
        store(spread, c, [0.5 * v for v in frame_sum(total, c, cols, main, base)])
    for g in range(count):
        store(spread, cols + g, [0.5 * v[None] for v in edge_sum(total, g, count, main, edge_base)])


def hidden_stencil(flags, spread, cond, cols, count, main, edge_h, here, start):
    halves = cond_halves(cond, main)
    for g in range(count):
        h = [half_silu(v + b) for v, b in zip(split_wide(spread, cols + g, 1, main), halves)]
        above = [lax.rem(rows_of(v), 2) == 1 for v in h]
        h = [
            jnp.where(jnp.where(a, flags[HAS_UP], flags[HAS_DOWN]) > 0, v, 0.0) for v, a in zip(h, above)
        ]
        store(edge_h, g, h)

    def column(c):
        return [half_silu(v + b) for v, b in zip(split_wide(spread, c, CHUNK, main), halves)]

    def edge(g):
        return [v[0] for v in split_wide(edge_h, g, 1, main)]

    inner_stencil(column, edge, cols, count, here, start)


def split_wide(ref, start, size, main):
    return [ref[start : start + size, :, :main], ref[start : start + size, :, main:]]


def residual(source, totals, cols, main, r, keep=None):
    for c in range(0, cols, CHUNK):
        x = source(c)
        sums = [frame_sum(total, c, cols, main, base) for total, base in totals]
        value = [x[0] + s[0] for s in sums] + [beside(x[1] + sums[0][1], x[1] + sums[1][1])]
        lane, size = 0, CHUNK * SUB
        for v in value:
            width = v.shape[-1]
            v = v.reshape(size, width)
            if keep is not None:
                v = jnp.where(keep, v, 0.0)
            r[c * SUB : c * SUB + size, lane : lane + width] = v.astype(BF16)
            lane += width


def second_convolution(flags, spread, conds, cols, count, main, weight, tails, edge_h, here, there, total):
    size, step = cols * SUB, cols * SUB + PAD

    @stage(flags)
    def _():
        hidden_stencil(flags, spread, conds[0], cols, count, main, edge_h.at[0], here, 0)

    @stage(flags)
    def _():
        convolve(here, weight, tails, total, 0, size, main)
        hidden_stencil(flags, spread, conds[1], cols, count, main, edge_h.at[1], there, 0)

    @stage(flags)
    def _():
        convolve(there, weight, tails, total, 0, size, main, step)

    return [(total, 0), (total, step)]


def columns(video, f, main):
    return lambda c, size=CHUNK: split(video[f, c : c + size].astype(F32), main)


def prepare_kernel(main, flags, raw, video, edge, sent):
    cols = video.shape[1]
    half, count = cols // 2, cols // 4
    for f in range(2):
        for c in range(0, cols, CHUNK):
            store(video.at[f], c, split(raw[f, c : c + CHUNK], main))
    far = columns(video, flags[FAR], main)
    for c in range(0, half, CHUNK):
        low, high = far(c), far(half + c)
        value = jnp.concatenate([low[0], high[0], beside(low[1], high[1])], axis=-1)
        sent[c : c + CHUNK] = value.astype(BF16)
    for i, which in enumerate((NEAR, FAR)):
        column = columns(video, flags[which], main)
        tile = edges_of(lambda c: [v[0] for v in column(c, 1)], count)
        for g in range(count):
            for k, value in enumerate(tile(g)):
                store(edge, (2 * k + i) * count + g, [v[None] for v in value])


def first_stencil(flags, video, which, slot, own, up, down, main, here):
    cols = video.shape[1]
    count, step = cols // 4, cols * SUB + PAD
    slots = own.shape[0] // (2 * count)

    def at(ref):
        return lambda k, g: [v[0] for v in split(ref[pl.ds((slots * k + slot) * count + g, 1)].astype(F32), main)]

    nearby = edge_stencil(flags, lambda g: at(own)(0, g), at(up), at(down), count, main, here, step)
    inner_stencil(columns(video, flags[which], main), lambda g: nearby[g], cols, count, here)


def near_kernel(
    main, flags, video, own, up, down, start, end, first, second,
    r, tails_first, tails_second, here, there, total, spread, edge_h,
):
    cols = video.shape[1]
    count, step = cols // 4, cols * SUB + PAD
    rows = step + (count + count % 2) * SUB

    pack_tails(first, tails_first, main)
    first_stencil(flags, video, NEAR, 0, own, up, down, main, here)

    pack_tails(second, tails_second, main)

    @stage(flags)
    def _():
        convolve(here, first, tails_first, total, 0, rows, main)

    spread_halves(total, spread, cols, count, main, 0, step)
    totals = second_convolution(
        flags, spread, (start, end), cols, count, main, second, tails_second, edge_h, here, there, total
    )
    residual(columns(video, flags[NEAR], main), totals, cols, main, r)


def relay_kernel(main, got, edge):
    half = got.shape[0]
    count = half // 2
    tile = edges_of(lambda c: [v[0] for v in unpack(got[c % half : c % half + 1].astype(F32), main, c // half)], count)
    for g in range(count):
        for k, value in enumerate(tile(g)):
            store(edge, k * count + g, [v[None] for v in value])


def got_columns(got, main):
    half = got.shape[0]
    return lambda c: unpack(got[c % half : c % half + CHUNK].astype(F32), main, c // half)


def other_kernel(
    main, flags, video, own, up, down, start, end, first, tails_first, second, tails_second,
    r, here, there, total, spread, edge_h,
):
    cols = video.shape[1]
    count, step = cols // 4, cols * SUB + PAD
    rows = step + (count + count % 2) * SUB
    first_stencil(flags, video, FAR, 1, own, up, down, main, here)

    @stage(flags)
    def _():
        convolve(here, first, tails_first, total, 0, rows, main)

    spread_halves(total, spread, cols, count, main, 0, step)

    totals = second_convolution(
        flags, spread, (start, end), cols, count, main, second, tails_second, edge_h, here, there, total
    )
    residual(columns(video, flags[FAR], main), totals, cols, main, r)


def mix(sources, taps, main, p):
    left = [r[:, p * main : (p + 1) * main] for r, _ in sources] + [r[:, 2 * main :] for r, _ in sources]
    right = [taps[t, :main] for _, t in sources]
    for _, t in sources:
        tail = taps[t, main:]
        right += [tail, jnp.zeros_like(tail)] if p == 0 else [jnp.zeros_like(tail), tail]
    return jnp.dot(jnp.concatenate(left, axis=1), jnp.concatenate(right, axis=0), preferred_element_type=F32)


def blend(r, mixed, start, size, main):
    value = r[start : start + size].astype(F32)
    both = [unpack(value, main, p) for p in range(2)]
    out = []
    for i in range(2):
        part = None
        for p in range(2):
            t = 0.5 * mixed(p, start, size)[i]
            term = both[p][i] + half_silu(t)
            part = term if part is None else part + term
        out.append(0.5 * part)
    return out


def far_kernel(
    main, flags, got, own, up, down, start, end, first, tails_first, second, tails_second, r_near, r_far, taps,
    out, mixed, here, there, total, spread, edge_h, r, sums,
):
    half = got.shape[0]
    cols = 2 * half
    count, size = half // 2, cols * SUB
    step = size + PAD
    rows = step + (count + count % 2) * SUB

    def at(ref):
        return lambda k, g: [v[0] for v in split(ref[k * count + g : k * count + g + 1].astype(F32), main)]

    nearby = edge_stencil(flags, lambda g: at(own)(0, g), at(up), at(down), count, main, here, step)
    inner_stencil(got_columns(got, main), lambda g: nearby[g], cols, count, here)
    convolve(here, first, tails_first, total, 0, rows, main)
    spread_halves(total, spread, cols, count, main, 0, step)
    to_far, to_near = flags[TAP_FAR], flags[TAP_NEAR]
    toward = [(to_far, to_near), (to_near, to_far)]
    totals = second_convolution(
        flags, spread, (start, end), cols, count, main, second, tails_second, edge_h, here, there, total
    )

    @stage(flags)
    def _():
        for p in range(2):
            mixed[p] = mix([(r_far, toward[p][0]), (r_near, 1)], taps, main, p)
        residual(got_columns(got, main), totals, cols, main, r, flags[HAS_FAR] > 0)

    @stage(flags)
    def _():
        for p in range(2):
            sums[p] = mix([(r, toward[p][0]), (r_far, 1), (r_near, toward[p][1])], taps, main, p)

    piece = CHUNK * SUB
    for s in range(0, size, piece):
        value = blend(r_far, lambda p, a, n: split(sums[p, a : a + n], main), s, piece, main)
        store(out, s // SUB, [v.reshape(CHUNK, SUB, v.shape[-1]) for v in value])


def last_kernel(main, parts, flags, got, mixed, r_near, taps, done, out, staged, sums, sems):
    cols = done.shape[0]
    copies = [pltpu.make_async_copy(done, out.at[flags[FAR]], sems.at[parts])]
    copies[0].start()
    toward = [flags[TAP_NEAR], flags[TAP_FAR]]
    for p in range(2):
        sums[p] = mixed[p] + mix([(got, toward[p])], taps, main, p)
    piece = CHUNK * SUB
    for i in range(parts):
        first, last = i * cols // parts, (i + 1) * cols // parts

        @stage(flags)
        def _():
            for c in range(first, last, CHUNK):
                value = blend(r_near, lambda p, a, n: split(sums[p, a : a + n], main), c * SUB, piece, main)
                store(staged, c, [v.reshape(CHUNK, SUB, v.shape[-1]) for v in value])

        copy = pltpu.make_async_copy(
            staged.at[first:last], out.at[flags[NEAR], first:last], sems.at[i]
        )
        copy.start()
        copies.append(copy)
    for copy in copies:
        copy.wait()


VMEM = pl.BlockSpec(memory_space=pltpu.VMEM)
SMEM = pl.BlockSpec(memory_space=pltpu.SMEM)
HBM = pl.BlockSpec(memory_space=pltpu.HBM)


def call(kernel, outs, args, scratch=(), name=None, flops=0, out_specs=None, limit=24):
    return pl.pallas_call(
        kernel,
        out_shape=outs,
        in_specs=[SMEM if a.dtype == jnp.int32 else VMEM for a in args],
        out_specs=out_specs or jax.tree.map(lambda _: VMEM, outs),
        scratch_shapes=list(scratch),
        name=name,
        cost_estimate=pl.CostEstimate(flops=flops, bytes_accessed=1 << 20, transcendentals=0),
        compiler_params=pltpu.CompilerParams(vmem_limit_bytes=limit << 20),
    )(*args)


def pairs(count, start):
    links = [(i, i + 1) for i in range(start, count - 1, 2)]
    return links + [(b, a) for a, b in links]


def row_neighbours(edge):
    count = lax.axis_size("row")
    if count == 1:
        return edge, edge
    first = lax.ppermute(edge, "row", pairs(count, 0))
    if count == 2:
        return first, first
    second = lax.ppermute(edge, "row", pairs(count, 1))
    even = lax.axis_index("row") % 2 == 0
    return jnp.where(even, second, first), jnp.where(even, first, second)


def shards(latents, conv_first, conv_second, conv_time, cond_start, cond_end):
    _, rows, cols, channels = latents.shape
    main = channels // LANES * LANES
    assert latents.shape[0] == 2 and rows == SUB and 2 * (channels - main) == LANES and cols % 4 == 0
    pixels, count = rows * cols, cols // 4
    step = pixels + PAD
    width = 3 * main + 2 * LANES
    wide = main + 2 * LANES
    packed = 2 * main + LANES
    frames_n, rows_n = lax.axis_size("frame"), lax.axis_size("row")
    frame, row = lax.axis_index("frame"), lax.axis_index("row")
    odd = frame % 2
    has_far = jnp.where(odd == 1, frame < frames_n - 1, frame > 0)
    flags = jnp.stack([1 - odd, odd, 2 * odd, 2 - 2 * odd, has_far, row > 0, row < rows_n - 1]).astype(jnp.int32)
    video = jnp.transpose(latents, (0, 2, 1, 3))
    unit = 32 * pixels * LANES * LANES

    def struct(*shape, dtype=BF16):
        return jax.ShapeDtypeStruct(shape, dtype)

    here, there = (step + (count + 3) * SUB, width), (step, width)
    work = [
        pltpu.VMEM(here, BF16), pltpu.VMEM(there, BF16), pltpu.VMEM((2 * step, wide), F32),
        pltpu.VMEM((cols + count, SUB, main + LANES), F32), pltpu.VMEM((2, count, SUB, main + LANES), F32),
    ]
    video, edge, sent = call(
        functools.partial(prepare_kernel, main),
        (struct(2, cols, SUB, main + LANES), struct(4 * count, SUB, main + LANES), struct(cols // 2, SUB, packed)),
        (flags, video), name="prepare", flops=8 * unit,
    )
    up, down = row_neighbours(edge)
    got_far = lax.ppermute(sent, "frame", pairs(frames_n, 1))
    first, second, taps = conv_first, conv_second, conv_time
    r_near, tails_first, tails_second = call(
        functools.partial(near_kernel, main),
        (struct(pixels, packed), struct(width, 2 * LANES), struct(width, 2 * LANES)),
        (flags, video, edge, up, down, cond_start, cond_end, first, second), work, "near", 54 * unit,
    )
    got_near = lax.ppermute(r_near, "frame", pairs(frames_n, 0))
    got_far, _ = lax.optimization_barrier((got_far, r_near))
    far_edge = call(functools.partial(relay_kernel, main), struct(2 * count, SUB, main + LANES), (got_far,), name="relay")
    far_up, far_down = row_neighbours(far_edge)
    r_far = call(
        functools.partial(other_kernel, main), struct(pixels, packed),
        (flags, video, edge, up, down, cond_start, cond_end, first, tails_first, second, tails_second),
        work, "other", 54 * unit,
    )
    done, mixed = call(
        functools.partial(far_kernel, main), (struct(cols, SUB, channels), struct(2, pixels, channels, dtype=F32)),
        (
            flags, got_far, far_edge, far_up, far_down, cond_start, cond_end, first, tails_first, second,
            tails_second, r_near, r_far, taps,
        ),
        [*work, pltpu.VMEM((pixels, packed), BF16), pltpu.VMEM((2, pixels, channels), F32)], "far", 54 * unit,
    )
    parts = 3
    out = call(
        functools.partial(last_kernel, main, parts), struct(2, cols, SUB, channels),
        (flags, got_near, mixed, r_near, taps, done),
        [
            pltpu.VMEM((cols, SUB, channels), BF16), pltpu.VMEM((2, pixels, channels), F32),
            pltpu.SemaphoreType.DMA((parts + 1,)),
        ],
        "last", 4 * unit, HBM,
    )
    return jnp.transpose(out, (0, 2, 1, 3))


def solution(mesh):
    placed = (P("frame", "row", None, None), P(), P(), P(), P(), P())
    return jax.shard_map(
        shards, mesh=mesh, in_specs=placed, out_specs=P("frame", "row", None, None), check_vma=False
    )
```

```python
import functools

import jax
import jax.numpy as jnp
from jax import lax
from jax.experimental import pallas as pl
from jax.experimental.pallas import tpu as pltpu
from jax.sharding import PartitionSpec as P

F32 = jnp.float32
BF16 = jnp.bfloat16
LANES = 128
HALF = LANES // 2
SUB = 8
CHUNK = 2
PAD = 2 * SUB

NEAR, FAR, TAP_FAR, TAP_NEAR, HAS_FAR, HAS_UP, HAS_DOWN = range(7)


def split(value, main):
    tail = value[..., main:]
    if tail.shape[-1] < LANES:
        tail = jnp.concatenate([tail, jnp.zeros_like(tail)], axis=-1)
    return [value[..., :main], tail]


def rows_of(value):
    return lax.broadcasted_iota(jnp.int32, value.shape, value.ndim - 2)


def lanes_of(value):
    return lax.broadcasted_iota(jnp.int32, value.shape, value.ndim - 1)


def turn(value, shift):
    shift %= value.shape[-2]
    return value if shift == 0 else pltpu.roll(value, shift, value.ndim - 2)


def swap_halves(value):
    return pltpu.roll(value, HALF, value.ndim - 1)


def beside(low, high):
    return jnp.where(lanes_of(low) < HALF, low, swap_halves(high))


def unpack(value, main, which):
    tail = value[..., 2 * main :]
    return [value[..., which * main : (which + 1) * main], swap_halves(tail) if which else tail]


def store(ref, start, value):
    main, tail = value
    width = main.shape[-1]
    ref[pl.ds(start, main.shape[0]), :, :width] = main.astype(ref.dtype)
    ref[pl.ds(start, main.shape[0]), :, width:] = tail[..., : ref.shape[-1] - width].astype(ref.dtype)


def edges_of(column, count):
    def tile(g):
        outer, second = None, None
        for j in range(4):
            x = column(j * count + g)
            z = [jnp.where(rows_of(v) == 7, turn(v, 1), turn(v, -1)) for v in x]
            x, z = [turn(v, 2 * j) for v in x], [turn(v, 2 * j) for v in z]
            if j == 0:
                outer, second = x, z
            else:
                at = lambda v: (rows_of(v) == (2 * j + 7) % 8) | (rows_of(v) == 2 * j)
                outer = [jnp.where(at(v), v, o) for v, o in zip(x, outer)]
                second = [jnp.where(at(v), v, o) for v, o in zip(z, second)]
        return outer, second

    return tile


class Stencil:
    def __init__(self, here, start=0):
        self.here = here
        self.row = start

    @staticmethod
    def pieces(prev, mid, nxt):
        return [prev[0], mid[0], nxt[0], beside(prev[1], mid[1]), nxt[1]]

    def put(self, pieces):
        size, lane = pieces[0].shape[0] * SUB, 0
        for piece in pieces:
            width = piece.shape[-1]
            self.here[self.row : self.row + size, lane : lane + width] = piece.reshape(size, width).astype(BF16)
            lane += width
        self.row += size


def pack_tails(weight, tails, main):
    row = 0
    for part in (slice(0, main), slice(main, None)):
        for a in range(3):
            left, mid, right = (weight[a, b, part, main:] for b in range(3))
            size = left.shape[0]
            tails[row : row + size, :LANES] = jnp.concatenate([left, mid], axis=1)
            tails[row : row + size, LANES:] = jnp.concatenate([right, jnp.zeros_like(right)], axis=1)
            row += size
    tails[row:] = jnp.zeros_like(tails[row:])


def convolve(here, weight, tails, total, start, size, main, into=0):
    def taps(column):
        parts = [weight[a, column, :main, :main] for a in range(3)] + [weight[a, column, main:, :main] for a in range(3)]
        return jnp.concatenate(parts + [jnp.zeros_like(parts[-1])], axis=0)

    def left(by):
        first = start + by * SUB
        return here[first : first + size]

    rows = slice(into, into + size)

    def two():
        total[rows, :main] = jnp.dot(left(1), taps(1), preferred_element_type=F32) + jnp.dot(
            left(0), taps(0), preferred_element_type=F32
        )

    def one():
        total[rows, main : 2 * main] = jnp.dot(left(2), taps(2), preferred_element_type=F32)

    def last():
        total[rows, 2 * main :] = jnp.dot(left(1), tails[...], preferred_element_type=F32)

    return [two, one, last]


def weave(some, others=()):
    for i, step in enumerate(some):
        step()
        for other in others[i * len(others) // len(some) : (i + 1) * len(others) // len(some)]:
            other()


def tail_of(left, mid, right):
    return left[..., :LANES] + swap_halves(mid[..., :LANES]) + right[..., LANES:]


def frame_sum(total, c, cols, main, base=0):
    out, tail = [], []
    for i in range(c, c + CHUNK):
        s = base + i * SUB
        mid = total[s : s + SUB, 2 * main :]
        left = total[s - SUB : s, 2 * main :] if i > 0 else jnp.zeros_like(mid)
        right = total[s + SUB : s + 2 * SUB, 2 * main :] if i < cols - 1 else jnp.zeros_like(mid)
        out.append(total[s : s + SUB, :main] + total[s : s + SUB, main : 2 * main])
        tail.append(tail_of(left, mid, right))
    return [jnp.stack(out), jnp.stack(tail)]


def edge_sum(total, g, count, main, base):
    def tile(i, part):
        return total[base + i * SUB : base + (i + 1) * SUB, part]

    tail = slice(2 * main, None)
    mid = tile(g, tail)
    row = rows_of(mid)
    left = tile(g - 1, tail) if g > 0 else jnp.where((row == 7) | (row == 0), 0.0, turn(tile(count - 1, tail), 2))
    right = tile(g + 1, tail) if g < count - 1 else jnp.where((row == 5) | (row == 6), 0.0, turn(tile(0, tail), -2))
    return [tile(g, slice(0, main)) + tile(g, slice(main, 2 * main)), tail_of(left, mid, right)]


def edge_stencil(flags, outer, up, down, count, main, here, start):
    nearby = []
    has_up, has_down = flags[HAS_UP] > 0, flags[HAS_DOWN] > 0

    def pieces(g):
        prev, mid, nxt = [], [], []
        ups, downs = [up(k, g) for k in range(2)], [down(k, g) for k in range(2)]
        own = outer(g)
        for i in range(2):
            above = lax.rem(rows_of(own[i]), 2) == 1
            crossed = jnp.where(above, turn(own[i], -1), turn(own[i], 1))
            u_out, u_sec = (jnp.where(has_up, ups[k][i], 0.0) for k in range(2))
            d_out, d_sec = (jnp.where(has_down, downs[k][i], 0.0) for k in range(2))
            prev.append(jnp.where(above, u_sec, crossed))
            mid.append(jnp.where(above, u_out, d_out))
            nxt.append(jnp.where(above, crossed, d_sec))
        nearby.append(mid)
        return [p[None] for p in Stencil.pieces(prev, mid, nxt)]

    def wrap(values, shift, first, last):
        return [jnp.where((rows_of(v) == first) | (rows_of(v) == last), 0.0, turn(v, shift)) for v in values]

    tiles = [pieces(g) for g in range(count)]
    before, after = wrap(tiles[-1], 2, 7, 0), wrap(tiles[0], -2, 5, 6)
    tiles = [before, *tiles, after]
    stencil = Stencil(here, start)
    for tile in tiles:
        stencil.put(tile)
    return nearby


def inner_stencil(column, edge, cols, count, here, start=0):
    stencil = Stencil(here, start)

    def add(c):
        mid = column(c)
        outer = [[turn(v, -2 * (i // count)) for v in edge(i % count)] for i in range(c, c + CHUNK)]
        prev, nxt = [], []
        for k, v in enumerate(mid):
            e = jnp.stack([o[k] for o in outer])
            prev.append(turn(jnp.where(rows_of(v) == 7, e, v), 1))
            nxt.append(turn(jnp.where(rows_of(v) == 0, e, v), -1))
        pieces = Stencil.pieces(prev, mid, nxt)
        if c == 0:
            stencil.put([jnp.zeros_like(p[:1]) for p in pieces])
        stencil.put(pieces)
        if c == cols - CHUNK:
            stencil.put([jnp.zeros_like(p[:1]) for p in pieces])

    return [functools.partial(add, c) for c in range(0, cols, CHUNK)]


def half_silu(y):
    return y + y * jnp.tanh(y)


def stage(flags):
    return pl.when(flags[NEAR] >= 0)


def cond_halves(cond, main):
    return [0.5 * v for v in split(cond[...].reshape(1, cond.shape[-1]), main)]


def spread_halves(total, spread, cols, count, main, base, edge_base):
    for c in range(0, cols, CHUNK):
        store(spread, c, [0.5 * v for v in frame_sum(total, c, cols, main, base)])
    for g in range(count):
        store(spread, cols + g, [0.5 * v[None] for v in edge_sum(total, g, count, main, edge_base)])


def hidden_stencil(flags, spread, cond, cols, count, main, edge_h, here, start):
    halves = cond_halves(cond, main)

    def outside(g):
        h = [half_silu(v + b) for v, b in zip(split_wide(spread, cols + g, 1, main), halves)]
        above = [lax.rem(rows_of(v), 2) == 1 for v in h]
        store(edge_h, g, [jnp.where(jnp.where(a, flags[HAS_UP], flags[HAS_DOWN]) > 0, v, 0.0) for v, a in zip(h, above)])

    def column(c):
        return [half_silu(v + b) for v, b in zip(split_wide(spread, c, CHUNK, main), halves)]

    def edge(g):
        return [v[0] for v in split_wide(edge_h, g, 1, main)]

    return [functools.partial(outside, g) for g in range(count)] + inner_stencil(column, edge, cols, count, here, start)


def split_wide(ref, start, size, main):
    return [ref[start : start + size, :, :main], ref[start : start + size, :, main:]]


def residual(source, totals, cols, main, r, keep=None):
    for c in range(0, cols, CHUNK):
        x = source(c)
        sums = [frame_sum(total, c, cols, main, base) for total, base in totals]
        value = [x[0] + s[0] for s in sums] + [beside(x[1] + sums[0][1], x[1] + sums[1][1])]
        lane, size = 0, CHUNK * SUB
        for v in value:
            width = v.shape[-1]
            v = v.reshape(size, width)
            if keep is not None:
                v = jnp.where(keep, v, 0.0)
            r[c * SUB : c * SUB + size, lane : lane + width] = v.astype(BF16)
            lane += width


def second_convolution(flags, spread, conds, cols, count, main, weight, tails, edge_h, here, total):
    step = cols * SUB + PAD
    for p in range(2):
        weave(hidden_stencil(flags, spread, conds[p], cols, count, main, edge_h.at[p], here, p * step))

    @stage(flags)
    def _():
        weave(convolve(here, weight, tails, total, 0, step + cols * SUB, main))

    return [(total, 0), (total, step)]


def columns(video, f, main):
    return lambda c, size=CHUNK: split(video[f, c : c + size].astype(F32), main)


def prepare_kernel(main, flags, raw, video, edge, sent):
    cols = video.shape[1]
    half, count = cols // 2, cols // 4
    for f in range(2):
        for c in range(0, cols, CHUNK):
            store(video.at[f], c, split(raw[f, c : c + CHUNK], main))
    far = columns(video, flags[FAR], main)
    for c in range(0, half, CHUNK):
        low, high = far(c), far(half + c)
        value = jnp.concatenate([low[0], high[0], beside(low[1], high[1])], axis=-1)
        sent[c : c + CHUNK] = value.astype(BF16)
    for i, which in enumerate((NEAR, FAR)):
        column = columns(video, flags[which], main)
        tile = edges_of(lambda c: [v[0] for v in column(c, 1)], count)
        for g in range(count):
            for k, value in enumerate(tile(g)):
                store(edge, (2 * k + i) * count + g, [v[None] for v in value])


def first_stencil(flags, video, which, slot, own, up, down, main, here):
    cols = video.shape[1]
    count, step = cols // 4, cols * SUB + PAD
    slots = own.shape[0] // (2 * count)

    def at(ref):
        return lambda k, g: [v[0] for v in split(ref[pl.ds((slots * k + slot) * count + g, 1)].astype(F32), main)]

    nearby = edge_stencil(flags, lambda g: at(own)(0, g), at(up), at(down), count, main, here, step)
    return inner_stencil(columns(video, flags[which], main), lambda g: nearby[g], cols, count, here)


def near_kernel(
    main, flags, video, own, up, down, start, end, first, second,
    r, tails_first, tails_second, here, total, spread, edge_h,
):
    cols = video.shape[1]
    count, step = cols // 4, cols * SUB + PAD
    rows = step + (count + count % 2) * SUB

    pack_tails(first, tails_first, main)
    weave(first_stencil(flags, video, NEAR, 0, own, up, down, main, here))

    pack_tails(second, tails_second, main)

    @stage(flags)
    def _():
        weave(convolve(here, first, tails_first, total, 0, rows, main))

    spread_halves(total, spread, cols, count, main, 0, step)
    totals = second_convolution(
        flags, spread, (start, end), cols, count, main, second, tails_second, edge_h, here, total
    )
    residual(columns(video, flags[NEAR], main), totals, cols, main, r)


def relay_kernel(main, got, edge):
    half = got.shape[0]
    count = half // 2
    tile = edges_of(lambda c: [v[0] for v in unpack(got[c % half : c % half + 1].astype(F32), main, c // half)], count)
    for g in range(count):
        for k, value in enumerate(tile(g)):
            store(edge, k * count + g, [v[None] for v in value])


def got_columns(got, main):
    half = got.shape[0]
    return lambda c: unpack(got[c % half : c % half + CHUNK].astype(F32), main, c // half)


def other_kernel(
    main, flags, video, own, up, down, start, end, first, tails_first, second, tails_second,
    r, here, total, spread, edge_h,
):
    cols = video.shape[1]
    count, step = cols // 4, cols * SUB + PAD
    rows = step + (count + count % 2) * SUB
    weave(first_stencil(flags, video, FAR, 1, own, up, down, main, here))

    @stage(flags)
    def _():
        weave(convolve(here, first, tails_first, total, 0, rows, main))

    spread_halves(total, spread, cols, count, main, 0, step)

    totals = second_convolution(
        flags, spread, (start, end), cols, count, main, second, tails_second, edge_h, here, total
    )
    residual(columns(video, flags[FAR], main), totals, cols, main, r)


def mix(sources, taps, main, p):
    left = [r[:, p * main : (p + 1) * main] for r, _ in sources] + [r[:, 2 * main :] for r, _ in sources]
    right = [taps[t, :main] for _, t in sources]
    for _, t in sources:
        tail = taps[t, main:]
        right += [tail, jnp.zeros_like(tail)] if p == 0 else [jnp.zeros_like(tail), tail]
    return jnp.dot(jnp.concatenate(left, axis=1), jnp.concatenate(right, axis=0), preferred_element_type=F32)


def mix_kernel(main, flags, r_near, r_far, taps, mixed):
    toward = [(flags[TAP_FAR], flags[TAP_NEAR]), (flags[TAP_NEAR], flags[TAP_FAR])]
    for p in range(2):
        to_far, to_near = toward[p]
        left = [r[:, part] for part in (slice(p * main, (p + 1) * main), slice(2 * main, None)) for r in (r_far, r_near)]

        pairs_of = [(taps[1], taps[to_far]), (taps[to_near], taps[1])]

        def right(column):
            parts = [column(a[:main], b[:main]) for a, b in pairs_of]
            for tail in [column(a[main:], b[main:]) for a, b in pairs_of]:
                blank = jnp.zeros_like(tail)
                parts += [tail, blank] if p == 0 else [blank, tail]
            return jnp.concatenate(parts, axis=0)

        value = jnp.concatenate(left, axis=1)
        columns_of = [
            lambda a, b: a[:, :main], lambda a, b: b[:, :main], lambda a, b: jnp.concatenate([a[:, main:], b[:, main:]], axis=1)
        ]
        for k, column in enumerate(columns_of):
            part = jnp.dot(value, right(column), preferred_element_type=F32)
            mixed[p, :, k * main : k * main + part.shape[1]] = part


def blend(r, mixed, start, size, main):
    value = r[start : start + size].astype(F32)
    both = [unpack(value, main, p) for p in range(2)]
    terms = [mixed(p, start, size) for p in range(2)]
    return [0.5 * sum(both[p][i] + half_silu(0.5 * terms[p][i]) for p in range(2)) for i in range(2)]


def joined(mixed, sums, main, which):
    def at(p, a, n):
        return [x + y for x, y in zip(unpack(mixed[p, a : a + n], main, which), split(sums[p, a : a + n], main))]

    return at


def far_kernel(
    main, flags, got, own, up, down, start, end, first, tails_first, second, tails_second, r_far, taps, mixed,
    out, here, total, spread, edge_h, r, sums,
):
    half = got.shape[0]
    cols = 2 * half
    count, size = half // 2, cols * SUB
    step = size + PAD
    rows = step + (count + count % 2) * SUB

    def at(ref):
        return lambda k, g: [v[0] for v in split(ref[k * count + g : k * count + g + 1].astype(F32), main)]

    nearby = edge_stencil(flags, lambda g: at(own)(0, g), at(up), at(down), count, main, here, step)
    weave(inner_stencil(got_columns(got, main), lambda g: nearby[g], cols, count, here))
    weave(convolve(here, first, tails_first, total, 0, rows, main))
    spread_halves(total, spread, cols, count, main, 0, step)
    toward = [flags[TAP_FAR], flags[TAP_NEAR]]
    totals = second_convolution(
        flags, spread, (start, end), cols, count, main, second, tails_second, edge_h, here, total
    )

    residual(got_columns(got, main), totals, cols, main, r, flags[HAS_FAR] > 0)

    @stage(flags)
    def _():
        for p in range(2):
            sums[p] = mix([(r, toward[p])], taps, main, p)

    piece = CHUNK * SUB
    for s in range(0, size, piece):
        value = blend(r_far, joined(mixed, sums, main, 0), s, piece, main)
        store(out, s // SUB, [v.reshape(CHUNK, SUB, v.shape[-1]) for v in value])


def last_kernel(main, parts, flags, got, mixed, r_near, taps, done, out, staged, sums, sems):
    cols = done.shape[0]
    copies = [pltpu.make_async_copy(done, out.at[flags[FAR]], sems.at[parts])]
    copies[0].start()
    toward = [flags[TAP_NEAR], flags[TAP_FAR]]
    for p in range(2):
        sums[p] = mix([(got, toward[p])], taps, main, p)
    piece = CHUNK * SUB
    for i in range(parts):
        first, last = i * cols // parts, (i + 1) * cols // parts

        for c in range(first, last, CHUNK):
            value = blend(r_near, joined(mixed, sums, main, 1), c * SUB, piece, main)
            store(staged, c, [v.reshape(CHUNK, SUB, v.shape[-1]) for v in value])

        copy = pltpu.make_async_copy(
            staged.at[first:last], out.at[flags[NEAR], first:last], sems.at[i]
        )
        copy.start()
        copies.append(copy)
    for copy in copies:
        copy.wait()


VMEM = pl.BlockSpec(memory_space=pltpu.VMEM)
SMEM = pl.BlockSpec(memory_space=pltpu.SMEM)
HBM = pl.BlockSpec(memory_space=pltpu.HBM)


def call(kernel, outs, args, scratch=(), name=None, flops=0, out_specs=None, limit=24):
    return pl.pallas_call(
        kernel,
        out_shape=outs,
        in_specs=[SMEM if a.dtype == jnp.int32 else VMEM for a in args],
        out_specs=out_specs or jax.tree.map(lambda _: VMEM, outs),
        scratch_shapes=list(scratch),
        name=name,
        cost_estimate=pl.CostEstimate(flops=flops, bytes_accessed=1 << 20, transcendentals=0),
        compiler_params=pltpu.CompilerParams(vmem_limit_bytes=limit << 20),
    )(*args)


def pairs(count, start):
    links = [(i, i + 1) for i in range(start, count - 1, 2)]
    return links + [(b, a) for a, b in links]


def row_neighbours(edge):
    count = lax.axis_size("row")
    if count == 1:
        return edge, edge
    first = lax.ppermute(edge, "row", pairs(count, 0))
    if count == 2:
        return first, first
    second = lax.ppermute(edge, "row", pairs(count, 1))
    even = lax.axis_index("row") % 2 == 0
    return jnp.where(even, second, first), jnp.where(even, first, second)


def shards(latents, conv_first, conv_second, conv_time, cond_start, cond_end):
    _, rows, cols, channels = latents.shape
    main = channels // LANES * LANES
    assert latents.shape[0] == 2 and rows == SUB and 2 * (channels - main) == LANES and cols % 4 == 0
    pixels, count = rows * cols, cols // 4
    step = pixels + PAD
    width = 3 * main + 2 * LANES
    wide = 2 * main + 2 * LANES
    packed = 2 * main + LANES
    frames_n, rows_n = lax.axis_size("frame"), lax.axis_size("row")
    frame, row = lax.axis_index("frame"), lax.axis_index("row")
    odd = frame % 2
    has_far = jnp.where(odd == 1, frame < frames_n - 1, frame > 0)
    flags = jnp.stack([1 - odd, odd, 2 * odd, 2 - 2 * odd, has_far, row > 0, row < rows_n - 1]).astype(jnp.int32)
    video = jnp.transpose(latents, (0, 2, 1, 3))
    unit = 32 * pixels * LANES * LANES

    def struct(*shape, dtype=BF16):
        return jax.ShapeDtypeStruct(shape, dtype)

    here = (2 * step + PAD, width)
    work = [
        pltpu.VMEM(here, BF16), pltpu.VMEM((2 * step, wide), F32),
        pltpu.VMEM((cols + count, SUB, main + LANES), F32), pltpu.VMEM((2, count, SUB, main + LANES), F32),
    ]
    video, edge, sent = call(
        functools.partial(prepare_kernel, main),
        (struct(2, cols, SUB, main + LANES), struct(4 * count, SUB, main + LANES), struct(cols // 2, SUB, packed)),
        (flags, video), name="prepare", flops=8 * unit,
    )
    up, down = row_neighbours(edge)
    got_far = lax.ppermute(sent, "frame", pairs(frames_n, 1))
    first, second, taps = conv_first, conv_second, conv_time
    r_near, tails_first, tails_second = call(
        functools.partial(near_kernel, main),
        (struct(pixels, packed), struct(width, 2 * LANES), struct(width, 2 * LANES)),
        (flags, video, edge, up, down, cond_start, cond_end, first, second), work, "near", 24 * unit,
    )
    got_near = lax.ppermute(r_near, "frame", pairs(frames_n, 0))
    r_far = call(
        functools.partial(other_kernel, main), struct(pixels, packed),
        (flags, video, edge, up, down, cond_start, cond_end, first, tails_first, second, tails_second),
        work, "other", 12 * unit,
    )
    got_far, r_far = lax.optimization_barrier((got_far, r_far))
    far_edge = call(functools.partial(relay_kernel, main), struct(2 * count, SUB, main + LANES), (got_far,), name="relay")
    far_up, far_down = row_neighbours(far_edge)
    mixed = call(
        functools.partial(mix_kernel, main), struct(2, pixels, packed, dtype=F32), (flags, r_near, r_far, taps),
        name="mix", flops=2 * unit,
    )
    done = call(
        functools.partial(far_kernel, main), struct(cols, SUB, channels),
        (
            flags, got_far, far_edge, far_up, far_down, cond_start, cond_end, first, tails_first, second, tails_second,
            r_far, taps, mixed,
        ),
        [*work, pltpu.VMEM((pixels, packed), BF16), pltpu.VMEM((2, pixels, channels), F32)], "far", 12 * unit,
    )
    parts = 3
    out = call(
        functools.partial(last_kernel, main, parts), struct(2, cols, SUB, channels),
        (flags, got_near, mixed, r_near, taps, done),
        [
            pltpu.VMEM((cols, SUB, channels), BF16), pltpu.VMEM((2, pixels, channels), F32),
            pltpu.SemaphoreType.DMA((parts + 1,)),
        ],
        "last", 4 * unit, HBM,
    )
    return jnp.transpose(out, (0, 2, 1, 3))


def solution(mesh):
    placed = (P("frame", "row", None, None), P(), P(), P(), P(), P())
    return jax.shard_map(
        shards, mesh=mesh, in_specs=placed, out_specs=P("frame", "row", None, None), check_vma=False
    )
```

```python
import functools

import jax
import jax.numpy as jnp
from jax import lax
from jax.experimental import pallas as pl
from jax.experimental.pallas import tpu as pltpu
from jax.sharding import PartitionSpec as P

F32 = jnp.float32
BF16 = jnp.bfloat16
LANES = 128
HALF = LANES // 2
SUB = 8
CHUNK = 2
PAD = 2 * SUB

NEAR, FAR, TAP_FAR, TAP_NEAR, HAS_FAR, HAS_UP, HAS_DOWN = range(7)


def split(value, main):
    tail = value[..., main:]
    if tail.shape[-1] < LANES:
        tail = jnp.concatenate([tail, jnp.zeros_like(tail)], axis=-1)
    return [value[..., :main], tail]


def rows_of(value):
    return lax.broadcasted_iota(jnp.int32, value.shape, value.ndim - 2)


def lanes_of(value):
    return lax.broadcasted_iota(jnp.int32, value.shape, value.ndim - 1)


def turn(value, shift):
    shift %= value.shape[-2]
    return value if shift == 0 else pltpu.roll(value, shift, value.ndim - 2)


def swap_halves(value):
    return pltpu.roll(value, HALF, value.ndim - 1)


def beside(low, high):
    return jnp.where(lanes_of(low) < HALF, low, swap_halves(high))


def unpack(value, main, which):
    tail = value[..., 2 * main :]
    return [value[..., which * main : (which + 1) * main], swap_halves(tail) if which else tail]


def store(ref, start, value):
    main, tail = value
    width = main.shape[-1]
    ref[pl.ds(start, main.shape[0]), :, :width] = main.astype(ref.dtype)
    ref[pl.ds(start, main.shape[0]), :, width:] = tail[..., : ref.shape[-1] - width].astype(ref.dtype)


def edges_of(column, count):
    def tile(g):
        outer, second = None, None
        for j in range(4):
            x = [turn(v, 2 * j) for v in column(j * count + g)]

            def place(old, above, below):
                if old is None:
                    return x
                return [
                    jnp.where((rows_of(v) == (2 * j + above) % 8) | (rows_of(v) == (2 * j + below) % 8), v, o)
                    for v, o in zip(x, old)
                ]

            outer, second = place(outer, 7, 0), place(second, 6, 1)
        return outer, second

    return tile


class Stencil:
    def __init__(self, here, start=0):
        self.here = here
        self.row = start

    @staticmethod
    def pieces(prev, mid, nxt):
        return [prev[0], mid[0], nxt[0], beside(prev[1], mid[1]), nxt[1]]

    def put(self, pieces):
        size, lane = pieces[0].shape[0] * SUB, 0
        for piece in pieces:
            width = piece.shape[-1]
            self.here[self.row : self.row + size, lane : lane + width] = piece.reshape(size, width).astype(BF16)
            lane += width
        self.row += size


def pack_tails(weight, tails, main):
    row = 0
    for part in (slice(0, main), slice(main, None)):
        for a in range(3):
            left, mid, right = (weight[a, b, part, main:] for b in range(3))
            size = left.shape[0]
            tails[row : row + size, :LANES] = jnp.concatenate([left, mid], axis=1)
            tails[row : row + size, LANES:] = jnp.concatenate([right, jnp.zeros_like(right)], axis=1)
            row += size
    tails[row:] = jnp.zeros_like(tails[row:])


def convolve(here, weight, tails, total, start, size, main, into=0):
    def taps(column):
        parts = [weight[a, column, :main, :main] for a in range(3)] + [weight[a, column, main:, :main] for a in range(3)]
        return jnp.concatenate(parts + [jnp.zeros_like(parts[-1])], axis=0)

    def left(by):
        first = start + by * SUB
        return here[first : first + size]

    rows = slice(into, into + size)

    def two():
        total[rows, :main] = jnp.dot(left(1), taps(1), preferred_element_type=F32) + jnp.dot(
            left(0), taps(0), preferred_element_type=F32
        )

    def one():
        total[rows, main : 2 * main] = jnp.dot(left(2), taps(2), preferred_element_type=F32)

    def last():
        total[rows, 2 * main :] = jnp.dot(left(1), tails[...], preferred_element_type=F32)

    return [two, one, last]


def weave(some, others=()):
    for i, step in enumerate(some):
        step()
        for other in others[i * len(others) // len(some) : (i + 1) * len(others) // len(some)]:
            other()


def tail_of(left, mid, right):
    return left[..., :LANES] + swap_halves(mid[..., :LANES]) + right[..., LANES:]


def frame_sum(total, c, cols, main, base=0):
    out, tail = [], []
    for i in range(c, c + CHUNK):
        s = base + i * SUB
        mid = total[s : s + SUB, 2 * main :]
        left = total[s - SUB : s, 2 * main :] if i > 0 else jnp.zeros_like(mid)
        right = total[s + SUB : s + 2 * SUB, 2 * main :] if i < cols - 1 else jnp.zeros_like(mid)
        out.append(total[s : s + SUB, :main] + total[s : s + SUB, main : 2 * main])
        tail.append(tail_of(left, mid, right))
    return [jnp.stack(out), jnp.stack(tail)]


def edge_sum(total, g, count, main, base):
    def tile(i, part):
        return total[base + i * SUB : base + (i + 1) * SUB, part]

    tail = slice(2 * main, None)
    mid = tile(g, tail)
    row = rows_of(mid)
    left = tile(g - 1, tail) if g > 0 else jnp.where((row == 7) | (row == 0), 0.0, turn(tile(count - 1, tail), 2))
    right = tile(g + 1, tail) if g < count - 1 else jnp.where((row == 5) | (row == 6), 0.0, turn(tile(0, tail), -2))
    return [tile(g, slice(0, main)) + tile(g, slice(main, 2 * main)), tail_of(left, mid, right)]


def edge_stencil(flags, outer, up, down, count, main, here, start):
    nearby = []
    has_up, has_down = flags[HAS_UP] > 0, flags[HAS_DOWN] > 0

    def pieces(g):
        prev, mid, nxt = [], [], []
        ups, downs = [up(k, g) for k in range(2)], [down(k, g) for k in range(2)]
        own = outer(g)
        for i in range(2):
            above = lax.rem(rows_of(own[i]), 2) == 1
            crossed = jnp.where(above, turn(own[i], -1), turn(own[i], 1))
            u_out, u_sec = (jnp.where(has_up, turn(ups[k][i], k), 0.0) for k in range(2))
            d_out, d_sec = (jnp.where(has_down, turn(downs[k][i], -k), 0.0) for k in range(2))
            prev.append(jnp.where(above, u_sec, crossed))
            mid.append(jnp.where(above, u_out, d_out))
            nxt.append(jnp.where(above, crossed, d_sec))
        nearby.append(mid)
        return [p[None] for p in Stencil.pieces(prev, mid, nxt)]

    def wrap(values, shift, first, last):
        return [jnp.where((rows_of(v) == first) | (rows_of(v) == last), 0.0, turn(v, shift)) for v in values]

    tiles = [pieces(g) for g in range(count)]
    before, after = wrap(tiles[-1], 2, 7, 0), wrap(tiles[0], -2, 5, 6)
    tiles = [before, *tiles, after]
    stencil = Stencil(here, start)
    for tile in tiles:
        stencil.put(tile)
    return nearby


def inner_stencil(column, edge, cols, count, here, start=0):
    stencil = Stencil(here, start)

    def add(c):
        mid = column(c)
        outer = [[turn(v, -2 * (i // count)) for v in edge(i % count)] for i in range(c, c + CHUNK)]
        prev, nxt = [], []
        for k, v in enumerate(mid):
            e = jnp.stack([o[k] for o in outer])
            prev.append(turn(jnp.where(rows_of(v) == 7, e, v), 1))
            nxt.append(turn(jnp.where(rows_of(v) == 0, e, v), -1))
        pieces = Stencil.pieces(prev, mid, nxt)
        if c == 0:
            stencil.put([jnp.zeros_like(p[:1]) for p in pieces])
        stencil.put(pieces)
        if c == cols - CHUNK:
            stencil.put([jnp.zeros_like(p[:1]) for p in pieces])

    return [functools.partial(add, c) for c in range(0, cols, CHUNK)]


def half_silu(y):
    return y + y * jnp.tanh(y)


def stage(flags):
    return pl.when(flags[NEAR] >= 0)


def cond_halves(cond, main):
    return [0.5 * v for v in split(cond[...].reshape(1, cond.shape[-1]), main)]


def spread_halves(total, spread, cols, count, main, base, edge_base):
    for c in range(0, cols, CHUNK):
        store(spread, c, [0.5 * v for v in frame_sum(total, c, cols, main, base)])
    for g in range(count):
        store(spread, cols + g, [0.5 * v[None] for v in edge_sum(total, g, count, main, edge_base)])


def hidden_stencil(flags, spread, cond, cols, count, main, edge_h, here, start):
    halves = cond_halves(cond, main)

    def outside(g):
        h = [half_silu(v + b) for v, b in zip(split_wide(spread, cols + g, 1, main), halves)]
        above = [lax.rem(rows_of(v), 2) == 1 for v in h]
        store(edge_h, g, [jnp.where(jnp.where(a, flags[HAS_UP], flags[HAS_DOWN]) > 0, v, 0.0) for v, a in zip(h, above)])

    def column(c):
        return [half_silu(v + b) for v, b in zip(split_wide(spread, c, CHUNK, main), halves)]

    def edge(g):
        return [v[0] for v in split_wide(edge_h, g, 1, main)]

    return [functools.partial(outside, g) for g in range(count)] + inner_stencil(column, edge, cols, count, here, start)


def split_wide(ref, start, size, main):
    return [ref[start : start + size, :, :main], ref[start : start + size, :, main:]]


def residual(source, totals, cols, main, r, keep=None):
    for c in range(0, cols, CHUNK):
        x = source(c)
        sums = [frame_sum(total, c, cols, main, base) for total, base in totals]
        value = [x[0] + s[0] for s in sums] + [beside(x[1] + sums[0][1], x[1] + sums[1][1])]
        lane, size = 0, CHUNK * SUB
        for v in value:
            width = v.shape[-1]
            v = v.reshape(size, width)
            if keep is not None:
                v = jnp.where(keep, v, 0.0)
            r[c * SUB : c * SUB + size, lane : lane + width] = v.astype(BF16)
            lane += width


def second_convolution(flags, spread, conds, cols, count, main, weight, tails, edge_h, here, total):
    step = cols * SUB + PAD
    for p in range(2):
        weave(hidden_stencil(flags, spread, conds[p], cols, count, main, edge_h.at[p], here, p * step))

    @stage(flags)
    def _():
        weave(convolve(here, weight, tails, total, 0, step + cols * SUB, main))

    return [(total, 0), (total, step)]


def columns(video, f, main):
    return lambda c, size=CHUNK: split(video[f, c : c + size].astype(F32), main)


def prepare_kernel(main, flags, raw, video, edge, sent):
    cols = video.shape[1]
    half, count = cols // 2, cols // 4
    for f in range(2):
        for c in range(0, cols, CHUNK):
            store(video.at[f], c, split(raw[f, c : c + CHUNK], main))
    far = columns(video, flags[FAR], main)
    for c in range(0, half, CHUNK):
        low, high = far(c), far(half + c)
        value = jnp.concatenate([low[0], high[0], beside(low[1], high[1])], axis=-1)
        sent[c : c + CHUNK] = value.astype(BF16)
    for i, which in enumerate((NEAR, FAR)):
        column = columns(video, flags[which], main)
        tile = edges_of(lambda c: [v[0] for v in column(c, 1)], count)
        for g in range(count):
            for k, value in enumerate(tile(g)):
                store(edge, (2 * k + i) * count + g, [v[None] for v in value])


def first_stencil(flags, video, which, slot, own, up, down, main, here):
    cols = video.shape[1]
    count, step = cols // 4, cols * SUB + PAD
    slots = own.shape[0] // (2 * count)

    def at(ref):
        return lambda k, g: [v[0] for v in split(ref[pl.ds((slots * k + slot) * count + g, 1)].astype(F32), main)]

    nearby = edge_stencil(flags, lambda g: at(own)(0, g), at(up), at(down), count, main, here, step)
    return inner_stencil(columns(video, flags[which], main), lambda g: nearby[g], cols, count, here)


def near_kernel(
    main, flags, video, own, up, down, start, end, first, second,
    r, tails_first, tails_second, here, total, spread, edge_h,
):
    cols = video.shape[1]
    count, step = cols // 4, cols * SUB + PAD
    rows = step + (count + count % 2) * SUB

    pack_tails(first, tails_first, main)
    weave(first_stencil(flags, video, NEAR, 0, own, up, down, main, here))

    pack_tails(second, tails_second, main)

    @stage(flags)
    def _():
        weave(convolve(here, first, tails_first, total, 0, rows, main))

    spread_halves(total, spread, cols, count, main, 0, step)
    totals = second_convolution(
        flags, spread, (start, end), cols, count, main, second, tails_second, edge_h, here, total
    )
    residual(columns(video, flags[NEAR], main), totals, cols, main, r)


def relay_kernel(main, got, edge):
    half = got.shape[0]
    count = half // 2
    tile = edges_of(lambda c: [v[0] for v in unpack(got[c % half : c % half + 1].astype(F32), main, c // half)], count)
    for g in range(count):
        for k, value in enumerate(tile(g)):
            store(edge, k * count + g, [v[None] for v in value])


def got_columns(got, main):
    half = got.shape[0]
    return lambda c: unpack(got[c % half : c % half + CHUNK].astype(F32), main, c // half)


def other_kernel(
    main, flags, video, own, up, down, start, end, first, tails_first, second, tails_second,
    total, here, spread, edge_h,
):
    cols = video.shape[1]
    count, step = cols // 4, cols * SUB + PAD
    rows = step + (count + count % 2) * SUB
    weave(first_stencil(flags, video, FAR, 1, own, up, down, main, here))

    @stage(flags)
    def _():
        weave(convolve(here, first, tails_first, total, 0, rows, main))

    spread_halves(total, spread, cols, count, main, 0, step)

    second_convolution(flags, spread, (start, end), cols, count, main, second, tails_second, edge_h, here, total)


def mix(sources, taps, main, p, rows=slice(None)):
    left = [r[rows, p * main : (p + 1) * main] for r, _ in sources] + [r[rows, 2 * main :] for r, _ in sources]
    right = [taps[t, :main] for _, t in sources]
    for _, t in sources:
        tail = taps[t, main:]
        right += [tail, jnp.zeros_like(tail)] if p == 0 else [jnp.zeros_like(tail), tail]
    return jnp.dot(jnp.concatenate(left, axis=1), jnp.concatenate(right, axis=0), preferred_element_type=F32)


def mix_kernel(main, flags, video, total, r_near, taps, r_far, mixed):
    cols = video.shape[1]
    toward = [(flags[TAP_FAR], flags[TAP_NEAR]), (flags[TAP_NEAR], flags[TAP_FAR])]

    def columns_of(a, b):
        return [a[:, :main], b[:, :main], jnp.concatenate([a[:, main:], b[:, main:]], axis=1)]

    def tails_of(p, a, b):
        parts = columns_of(a[main:], b[main:])
        blanks = [jnp.zeros_like(v) for v in parts]
        return [jnp.concatenate(v, axis=0) for v in (zip(parts, blanks) if p == 0 else zip(blanks, parts))]

    near = [
        [
            jnp.dot(r_near[:, p * main : (p + 1) * main], right, preferred_element_type=F32)
            for right in columns_of(taps[toward[p][1], :main], taps[1, :main])
        ]
        for p in range(2)
    ]
    residual(columns(video, flags[FAR], main), [(total, 0), (total, cols * SUB + PAD)], cols, main, r_far)
    for p in range(2):
        to_far, to_near = toward[p]
        left = jnp.concatenate([r_far[:, p * main : (p + 1) * main], r_far[:, 2 * main :], r_near[:, 2 * main :]], axis=1)
        rights = zip(
            columns_of(taps[1, :main], taps[to_far, :main]), tails_of(p, taps[1], taps[to_far]), tails_of(p, taps[to_near], taps[1])
        )
        for k, right in enumerate(rights):
            part = near[p][k] + jnp.dot(left, jnp.concatenate(right, axis=0), preferred_element_type=F32)
            mixed[p, :, k * main : k * main + part.shape[1]] = part


def blend(r, mixed, start, size, main):
    value = r[start : start + size].astype(F32)
    both = [unpack(value, main, p) for p in range(2)]
    terms = [mixed(p, start, size) for p in range(2)]
    return [0.5 * sum(both[p][i] + half_silu(0.5 * terms[p][i]) for p in range(2)) for i in range(2)]


def joined(mixed, sums, main, which):
    def at(p, a, n):
        return [x + y for x, y in zip(unpack(mixed[p, a : a + n], main, which), split(sums[p, a : a + n], main))]

    return at


def far_kernel(
    main, flags, got, own, up, down, start, end, first, tails_first, second, tails_second, r_far, taps, mixed,
    out, here, total, spread, edge_h, r, sums,
):
    half = got.shape[0]
    cols = 2 * half
    count, size = half // 2, cols * SUB
    step = size + PAD
    rows = step + (count + count % 2) * SUB

    def at(ref):
        return lambda k, g: [v[0] for v in split(ref[k * count + g : k * count + g + 1].astype(F32), main)]

    nearby = edge_stencil(flags, lambda g: at(own)(0, g), at(up), at(down), count, main, here, step)
    weave(inner_stencil(got_columns(got, main), lambda g: nearby[g], cols, count, here))
    weave(convolve(here, first, tails_first, total, 0, rows, main))
    spread_halves(total, spread, cols, count, main, 0, step)
    toward = [flags[TAP_FAR], flags[TAP_NEAR]]
    totals = second_convolution(
        flags, spread, (start, end), cols, count, main, second, tails_second, edge_h, here, total
    )

    residual(got_columns(got, main), totals, cols, main, r, flags[HAS_FAR] > 0)

    @stage(flags)
    def _():
        for p in range(2):
            sums[p] = mix([(r, toward[p])], taps, main, p)

    piece = CHUNK * SUB
    for s in range(0, size, piece):
        value = blend(r_far, joined(mixed, sums, main, 0), s, piece, main)
        store(out, s // SUB, [v.reshape(CHUNK, SUB, v.shape[-1]) for v in value])


def last_kernel(main, parts, flags, got, mixed, r_near, taps, done, out, staged, sums, sems):
    cols = done.shape[0]
    copies = [pltpu.make_async_copy(done, out.at[flags[FAR]], sems.at[parts])]
    copies[0].start()
    toward = [flags[TAP_NEAR], flags[TAP_FAR]]
    piece, halves = CHUNK * SUB, 2
    for i in range(parts):
        first, last = i * cols // parts, (i + 1) * cols // parts
        if i % (parts // halves) == 0:
            rows = slice(first * SUB, (first + cols // halves) * SUB)
            for p in range(2):
                sums[p, rows] = mix([(got, toward[p])], taps, main, p, rows)
        for c in range(first, last, CHUNK):
            value = blend(r_near, joined(mixed, sums, main, 1), c * SUB, piece, main)
            store(staged, c, [v.reshape(CHUNK, SUB, v.shape[-1]) for v in value])

        copy = pltpu.make_async_copy(
            staged.at[first:last], out.at[flags[NEAR], first:last], sems.at[i]
        )
        copy.start()
        copies.append(copy)
    for copy in copies:
        copy.wait()


VMEM = pl.BlockSpec(memory_space=pltpu.VMEM)
SMEM = pl.BlockSpec(memory_space=pltpu.SMEM)
HBM = pl.BlockSpec(memory_space=pltpu.HBM)


def call(kernel, outs, args, scratch=(), name=None, flops=0, out_specs=None, limit=24):
    return pl.pallas_call(
        kernel,
        out_shape=outs,
        in_specs=[SMEM if a.dtype == jnp.int32 else VMEM for a in args],
        out_specs=out_specs or jax.tree.map(lambda _: VMEM, outs),
        scratch_shapes=list(scratch),
        name=name,
        cost_estimate=pl.CostEstimate(flops=flops, bytes_accessed=1 << 20, transcendentals=0),
        compiler_params=pltpu.CompilerParams(vmem_limit_bytes=limit << 20),
    )(*args)


def pairs(count, start):
    links = [(i, i + 1) for i in range(start, count - 1, 2)]
    return links + [(b, a) for a, b in links]


def row_neighbours(edge):
    count = lax.axis_size("row")
    if count == 1:
        return edge, edge
    first = lax.ppermute(edge, "row", pairs(count, 0))
    if count == 2:
        return first, first
    second = lax.ppermute(edge, "row", pairs(count, 1))
    even = lax.axis_index("row") % 2 == 0
    return jnp.where(even, second, first), jnp.where(even, first, second)


def shards(latents, conv_first, conv_second, conv_time, cond_start, cond_end):
    _, rows, cols, channels = latents.shape
    main = channels // LANES * LANES
    assert latents.shape[0] == 2 and rows == SUB and 2 * (channels - main) == LANES and cols % 4 == 0
    pixels, count = rows * cols, cols // 4
    step = pixels + PAD
    width = 3 * main + 2 * LANES
    wide = 2 * main + 2 * LANES
    packed = 2 * main + LANES
    frames_n, rows_n = lax.axis_size("frame"), lax.axis_size("row")
    frame, row = lax.axis_index("frame"), lax.axis_index("row")
    odd = frame % 2
    has_far = jnp.where(odd == 1, frame < frames_n - 1, frame > 0)
    flags = jnp.stack([1 - odd, odd, 2 * odd, 2 - 2 * odd, has_far, row > 0, row < rows_n - 1]).astype(jnp.int32)
    video = jnp.transpose(latents, (0, 2, 1, 3))
    unit = 32 * pixels * LANES * LANES

    def struct(*shape, dtype=BF16):
        return jax.ShapeDtypeStruct(shape, dtype)

    here = (2 * step + PAD, width)
    work = [
        pltpu.VMEM(here, BF16), pltpu.VMEM((2 * step, wide), F32),
        pltpu.VMEM((cols + count, SUB, main + LANES), F32), pltpu.VMEM((2, count, SUB, main + LANES), F32),
    ]
    video, edge, sent = call(
        functools.partial(prepare_kernel, main),
        (struct(2, cols, SUB, main + LANES), struct(4 * count, SUB, main + LANES), struct(cols // 2, SUB, packed)),
        (flags, video), name="prepare", flops=8 * unit,
    )
    up, down = row_neighbours(edge)
    got_far = lax.ppermute(sent, "frame", pairs(frames_n, 1))
    first, second, taps = conv_first, conv_second, conv_time
    r_near, tails_first, tails_second = call(
        functools.partial(near_kernel, main),
        (struct(pixels, packed), struct(width, 2 * LANES), struct(width, 2 * LANES)),
        (flags, video, edge, up, down, cond_start, cond_end, first, second), work, "near", 24 * unit,
    )
    got_near = lax.ppermute(r_near, "frame", pairs(frames_n, 0))
    total_far = call(
        functools.partial(other_kernel, main), struct(2 * step, wide, dtype=F32),
        (flags, video, edge, up, down, cond_start, cond_end, first, tails_first, second, tails_second),
        [work[0], *work[2:]], "other", 12 * unit,
    )
    got_far, total_far = lax.optimization_barrier((got_far, total_far))
    far_edge = call(functools.partial(relay_kernel, main), struct(2 * count, SUB, main + LANES), (got_far,), name="relay")
    far_up, far_down = row_neighbours(far_edge)
    r_far, mixed = call(
        functools.partial(mix_kernel, main), (struct(pixels, packed), struct(2, pixels, packed, dtype=F32)),
        (flags, video, total_far, r_near, taps),
        name="mix", flops=2 * unit,
    )
    done = call(
        functools.partial(far_kernel, main), struct(cols, SUB, channels),
        (
            flags, got_far, far_edge, far_up, far_down, cond_start, cond_end, first, tails_first, second, tails_second,
            r_far, taps, mixed,
        ),
        [*work, pltpu.VMEM((pixels, packed), BF16), pltpu.VMEM((2, pixels, channels), F32)], "far", 12 * unit,
    )
    parts = 6
    out = call(
        functools.partial(last_kernel, main, parts), struct(2, cols, SUB, channels),
        (flags, got_near, mixed, r_near, taps, done),
        [
            pltpu.VMEM((cols, SUB, channels), BF16), pltpu.VMEM((2, pixels, channels), F32),
            pltpu.SemaphoreType.DMA((parts + 1,)),
        ],
        "last", 4 * unit, HBM,
    )
    return jnp.transpose(out, (0, 2, 1, 3))


def solution(mesh):
    placed = (P("frame", "row", None, None), P(), P(), P(), P(), P())
    return jax.shard_map(
        shards, mesh=mesh, in_specs=placed, out_specs=P("frame", "row", None, None), check_vma=False
    )
```

```python
import functools

import jax
import jax.numpy as jnp
from jax import lax
from jax.experimental import pallas as pl
from jax.experimental.pallas import tpu as pltpu
from jax.sharding import PartitionSpec as P

F32 = jnp.float32
BF16 = jnp.bfloat16
LANES = 128
HALF = LANES // 2
SUB = 8
CHUNK = 2
PAD = 2 * SUB

NEAR, FAR, TAP_FAR, TAP_NEAR, HAS_FAR, HAS_UP, HAS_DOWN = range(7)


def split(value, main):
    tail = value[..., main:]
    if tail.shape[-1] < LANES:
        tail = jnp.concatenate([tail, jnp.zeros_like(tail)], axis=-1)
    return [value[..., :main], tail]


def rows_of(value):
    return lax.broadcasted_iota(jnp.int32, value.shape, value.ndim - 2)


def lanes_of(value):
    return lax.broadcasted_iota(jnp.int32, value.shape, value.ndim - 1)


def turn(value, shift):
    shift %= value.shape[-2]
    return value if shift == 0 else pltpu.roll(value, shift, value.ndim - 2)


def swap_halves(value):
    return pltpu.roll(value, HALF, value.ndim - 1)


def beside(low, high):
    return jnp.where(lanes_of(low) < HALF, low, swap_halves(high))


def unpack(value, main, which):
    tail = value[..., 2 * main :]
    return [value[..., which * main : (which + 1) * main], swap_halves(tail) if which else tail]


def store(ref, start, value):
    main, tail = value
    width = main.shape[-1]
    ref[pl.ds(start, main.shape[0]), :, :width] = main.astype(ref.dtype)
    ref[pl.ds(start, main.shape[0]), :, width:] = tail[..., : ref.shape[-1] - width].astype(ref.dtype)


def edges_of(column, count):
    def tile(g):
        outer, second = None, None
        for j in range(4):
            x = [turn(v, 2 * j) for v in column(j * count + g)]

            def place(old, above, below):
                if old is None:
                    return x
                return [
                    jnp.where((rows_of(v) == (2 * j + above) % 8) | (rows_of(v) == (2 * j + below) % 8), v, o)
                    for v, o in zip(x, old)
                ]

            outer, second = place(outer, 7, 0), place(second, 6, 1)
        return outer, second

    return tile


class Stencil:
    def __init__(self, here, start=0):
        self.here = here
        self.row = start

    @staticmethod
    def pieces(prev, mid, nxt):
        return [prev[0], mid[0], nxt[0], beside(prev[1], mid[1]), nxt[1]]

    def put(self, pieces):
        size, lane = pieces[0].shape[0] * SUB, 0
        for piece in pieces:
            width = piece.shape[-1]
            self.here[self.row : self.row + size, lane : lane + width] = piece.reshape(size, width).astype(BF16)
            lane += width
        self.row += size


def pack_tails(weight, tails, main):
    row = 0
    for part in (slice(0, main), slice(main, None)):
        for a in range(3):
            left, mid, right = (weight[a, b, part, main:] for b in range(3))
            size = left.shape[0]
            tails[row : row + size, :LANES] = jnp.concatenate([left, mid], axis=1)
            tails[row : row + size, LANES:] = jnp.concatenate([right, jnp.zeros_like(right)], axis=1)
            row += size
    tails[row:] = jnp.zeros_like(tails[row:])


def convolve(here, weight, tails, total, start, size, main, into=0):
    def taps(column):
        parts = [weight[a, column, :main, :main] for a in range(3)] + [weight[a, column, main:, :main] for a in range(3)]
        return jnp.concatenate(parts + [jnp.zeros_like(parts[-1])], axis=0)

    def left(by):
        first = start + by * SUB
        return here[first : first + size]

    rows = slice(into, into + size)

    def two():
        total[rows, :main] = jnp.dot(left(1), taps(1), preferred_element_type=F32) + jnp.dot(
            left(0), taps(0), preferred_element_type=F32
        )

    def one():
        total[rows, main : 2 * main] = jnp.dot(left(2), taps(2), preferred_element_type=F32)

    def last():
        total[rows, 2 * main :] = jnp.dot(left(1), tails[...], preferred_element_type=F32)

    return [two, one, last]


def weave(some, others=()):
    for i, step in enumerate(some):
        step()
        for other in others[i * len(others) // len(some) : (i + 1) * len(others) // len(some)]:
            other()


def tail_of(left, mid, right):
    return left[..., :LANES] + swap_halves(mid[..., :LANES]) + right[..., LANES:]


def frame_sum(total, c, cols, main, base=0):
    out, tail = [], []
    for i in range(c, c + CHUNK):
        s = base + i * SUB
        mid = total[s : s + SUB, 2 * main :]
        left = total[s - SUB : s, 2 * main :] if i > 0 else jnp.zeros_like(mid)
        right = total[s + SUB : s + 2 * SUB, 2 * main :] if i < cols - 1 else jnp.zeros_like(mid)
        out.append(total[s : s + SUB, :main] + total[s : s + SUB, main : 2 * main])
        tail.append(tail_of(left, mid, right))
    return [jnp.stack(out), jnp.stack(tail)]


def edge_sum(total, g, count, main, base):
    def tile(i, part):
        return total[base + i * SUB : base + (i + 1) * SUB, part]

    tail = slice(2 * main, None)
    mid = tile(g, tail)
    row = rows_of(mid)
    left = tile(g - 1, tail) if g > 0 else jnp.where((row == 7) | (row == 0), 0.0, turn(tile(count - 1, tail), 2))
    right = tile(g + 1, tail) if g < count - 1 else jnp.where((row == 5) | (row == 6), 0.0, turn(tile(0, tail), -2))
    return [tile(g, slice(0, main)) + tile(g, slice(main, 2 * main)), tail_of(left, mid, right)]


def edge_stencil(flags, outer, up, down, count, main, here, start):
    nearby = []
    has_up, has_down = flags[HAS_UP] > 0, flags[HAS_DOWN] > 0

    def pieces(g):
        prev, mid, nxt = [], [], []
        ups, downs = [up(k, g) for k in range(2)], [down(k, g) for k in range(2)]
        own = outer(g)
        for i in range(2):
            above = lax.rem(rows_of(own[i]), 2) == 1
            crossed = jnp.where(above, turn(own[i], -1), turn(own[i], 1))
            u_out, u_sec = (jnp.where(has_up, turn(ups[k][i], k), 0.0) for k in range(2))
            d_out, d_sec = (jnp.where(has_down, turn(downs[k][i], -k), 0.0) for k in range(2))
            prev.append(jnp.where(above, u_sec, crossed))
            mid.append(jnp.where(above, u_out, d_out))
            nxt.append(jnp.where(above, crossed, d_sec))
        nearby.append(mid)
        return [p[None] for p in Stencil.pieces(prev, mid, nxt)]

    def wrap(values, shift, first, last):
        return [jnp.where((rows_of(v) == first) | (rows_of(v) == last), 0.0, turn(v, shift)) for v in values]

    tiles = [pieces(g) for g in range(count)]
    before, after = wrap(tiles[-1], 2, 7, 0), wrap(tiles[0], -2, 5, 6)
    tiles = [before, *tiles, after]
    stencil = Stencil(here, start)
    for tile in tiles:
        stencil.put(tile)
    return nearby


def inner_stencil(column, edge, cols, count, here, start=0):
    stencil = Stencil(here, start)

    def add(c):
        mid = column(c)
        outer = [[turn(v, -2 * (i // count)) for v in edge(i % count)] for i in range(c, c + CHUNK)]
        prev, nxt = [], []
        for k, v in enumerate(mid):
            e = jnp.stack([o[k] for o in outer])
            prev.append(turn(jnp.where(rows_of(v) == 7, e, v), 1))
            nxt.append(turn(jnp.where(rows_of(v) == 0, e, v), -1))
        pieces = Stencil.pieces(prev, mid, nxt)
        if c == 0:
            stencil.put([jnp.zeros_like(p[:1]) for p in pieces])
        stencil.put(pieces)
        if c == cols - CHUNK:
            stencil.put([jnp.zeros_like(p[:1]) for p in pieces])

    return [functools.partial(add, c) for c in range(0, cols, CHUNK)]


def half_silu(y):
    return y + y * jnp.tanh(y)


def stage(flags):
    return pl.when(flags[NEAR] >= 0)


def cond_halves(cond, main):
    return [0.5 * v for v in split(cond[...].reshape(1, cond.shape[-1]), main)]


def spread_halves(total, spread, cols, count, main, base, edge_base):
    for c in range(0, cols, CHUNK):
        store(spread, c, [0.5 * v for v in frame_sum(total, c, cols, main, base)])
    for g in range(count):
        store(spread, cols + g, [0.5 * v[None] for v in edge_sum(total, g, count, main, edge_base)])


def hidden_stencil(flags, spread, cond, cols, count, main, edge_h, here, start):
    halves = cond_halves(cond, main)

    def outside(g):
        h = [half_silu(v + b) for v, b in zip(split_wide(spread, cols + g, 1, main), halves)]
        above = [lax.rem(rows_of(v), 2) == 1 for v in h]
        store(edge_h, g, [jnp.where(jnp.where(a, flags[HAS_UP], flags[HAS_DOWN]) > 0, v, 0.0) for v, a in zip(h, above)])

    def column(c):
        return [half_silu(v + b) for v, b in zip(split_wide(spread, c, CHUNK, main), halves)]

    def edge(g):
        return [v[0] for v in split_wide(edge_h, g, 1, main)]

    return [functools.partial(outside, g) for g in range(count)] + inner_stencil(column, edge, cols, count, here, start)


def split_wide(ref, start, size, main):
    return [ref[start : start + size, :, :main], ref[start : start + size, :, main:]]


def residual(source, totals, cols, main, r, keep=None):
    for c in range(0, cols, CHUNK):
        x = source(c)
        sums = [frame_sum(total, c, cols, main, base) for total, base in totals]
        value = [x[0] + s[0] for s in sums] + [beside(x[1] + sums[0][1], x[1] + sums[1][1])]
        lane, size = 0, CHUNK * SUB
        for v in value:
            width = v.shape[-1]
            v = v.reshape(size, width)
            if keep is not None:
                v = jnp.where(keep, v, 0.0)
            r[c * SUB : c * SUB + size, lane : lane + width] = v.astype(BF16)
            lane += width


def second_convolution(flags, spread, conds, cols, count, main, weight, tails, edge_h, here, total):
    step = cols * SUB + PAD
    for p in range(2):
        weave(hidden_stencil(flags, spread, conds[p], cols, count, main, edge_h.at[p], here, p * step))

    @stage(flags)
    def _():
        weave(convolve(here, weight, tails, total, 0, step + cols * SUB, main))

    return [(total, 0), (total, step)]


def columns(video, f, main):
    return lambda c, size=CHUNK: split(video[f, c : c + size].astype(F32), main)


def prepare_kernel(main, flags, raw, video, edge, sent):
    cols = video.shape[1]
    half, count = cols // 2, cols // 4
    for f in range(2):
        for c in range(0, cols, CHUNK):
            store(video.at[f], c, split(raw[f, c : c + CHUNK], main))
    far = columns(video, flags[FAR], main)
    for c in range(0, half, CHUNK):
        low, high = far(c), far(half + c)
        value = jnp.concatenate([low[0], high[0], beside(low[1], high[1])], axis=-1)
        sent[c : c + CHUNK] = value.astype(BF16)
    for i, which in enumerate((NEAR, FAR)):
        column = columns(video, flags[which], main)
        tile = edges_of(lambda c: [v[0] for v in column(c, 1)], count)
        for g in range(count):
            for k, value in enumerate(tile(g)):
                store(edge, (2 * k + i) * count + g, [v[None] for v in value])


def first_stencil(flags, video, which, slot, own, up, down, main, here):
    cols = video.shape[1]
    count, step = cols // 4, cols * SUB + PAD
    slots = own.shape[0] // (2 * count)

    def at(ref):
        return lambda k, g: [v[0] for v in split(ref[pl.ds((slots * k + slot) * count + g, 1)].astype(F32), main)]

    nearby = edge_stencil(flags, lambda g: at(own)(0, g), at(up), at(down), count, main, here, step)
    return inner_stencil(columns(video, flags[which], main), lambda g: nearby[g], cols, count, here)


def near_kernel(
    main, flags, video, own, up, down, start, end, first, second,
    r, tails_first, tails_second, here, total, spread, edge_h,
):
    cols = video.shape[1]
    count, step = cols // 4, cols * SUB + PAD
    rows = step + (count + count % 2) * SUB

    pack_tails(first, tails_first, main)
    weave(first_stencil(flags, video, NEAR, 0, own, up, down, main, here))

    pack_tails(second, tails_second, main)

    @stage(flags)
    def _():
        weave(convolve(here, first, tails_first, total, 0, rows, main))

    spread_halves(total, spread, cols, count, main, 0, step)
    totals = second_convolution(
        flags, spread, (start, end), cols, count, main, second, tails_second, edge_h, here, total
    )
    residual(columns(video, flags[NEAR], main), totals, cols, main, r)


def relay_kernel(main, got, edge):
    half = got.shape[0]
    count = half // 2
    tile = edges_of(lambda c: [v[0] for v in unpack(got[c % half : c % half + 1].astype(F32), main, c // half)], count)
    for g in range(count):
        for k, value in enumerate(tile(g)):
            store(edge, k * count + g, [v[None] for v in value])


def got_columns(got, main):
    half = got.shape[0]
    return lambda c: unpack(got[c % half : c % half + CHUNK].astype(F32), main, c // half)


def other_kernel(
    main, flags, video, own, up, down, start, end, first, tails_first, second, tails_second,
    total, here, spread, edge_h,
):
    cols = video.shape[1]
    count, step = cols // 4, cols * SUB + PAD
    rows = step + (count + count % 2) * SUB
    weave(first_stencil(flags, video, FAR, 1, own, up, down, main, here))

    @stage(flags)
    def _():
        weave(convolve(here, first, tails_first, total, 0, rows, main))

    spread_halves(total, spread, cols, count, main, 0, step)

    second_convolution(flags, spread, (start, end), cols, count, main, second, tails_second, edge_h, here, total)


def mix(sources, taps, main, p, rows=slice(None)):
    left = [r[rows, p * main : (p + 1) * main] for r, _ in sources] + [r[rows, 2 * main :] for r, _ in sources]
    right = [taps[t, :main] for _, t in sources]
    for _, t in sources:
        tail = taps[t, main:]
        right += [tail, jnp.zeros_like(tail)] if p == 0 else [jnp.zeros_like(tail), tail]
    return jnp.dot(jnp.concatenate(left, axis=1), jnp.concatenate(right, axis=0), preferred_element_type=F32)


def mix_kernel(main, flags, video, total, r_near, taps, r_far, mixed):
    cols = video.shape[1]
    toward = [(flags[TAP_FAR], flags[TAP_NEAR]), (flags[TAP_NEAR], flags[TAP_FAR])]

    def columns_of(a, b):
        return [a[:, :main], b[:, :main], jnp.concatenate([a[:, main:], b[:, main:]], axis=1)]

    def tails_of(p, a, b):
        parts = columns_of(a[main:], b[main:])
        blanks = [jnp.zeros_like(v) for v in parts]
        return [jnp.concatenate(v, axis=0) for v in (zip(parts, blanks) if p == 0 else zip(blanks, parts))]

    near = [
        [
            jnp.dot(r_near[:, p * main : (p + 1) * main], right, preferred_element_type=F32)
            for right in columns_of(taps[toward[p][1], :main], taps[1, :main])
        ]
        for p in range(2)
    ]
    residual(columns(video, flags[FAR], main), [(total, 0), (total, cols * SUB + PAD)], cols, main, r_far)
    for p in range(2):
        to_far, to_near = toward[p]
        left = jnp.concatenate([r_far[:, p * main : (p + 1) * main], r_far[:, 2 * main :], r_near[:, 2 * main :]], axis=1)
        rights = zip(
            columns_of(taps[1, :main], taps[to_far, :main]), tails_of(p, taps[1], taps[to_far]), tails_of(p, taps[to_near], taps[1])
        )
        for k, right in enumerate(rights):
            part = near[p][k] + jnp.dot(left, jnp.concatenate(right, axis=0), preferred_element_type=F32)
            mixed[p, :, k * main : k * main + part.shape[1]] = part


def blend(r, mixed, start, size, main):
    value = r[start : start + size].astype(F32)
    both = [unpack(value, main, p) for p in range(2)]
    terms = [mixed(p, start, size) for p in range(2)]
    return [0.5 * sum(both[p][i] + half_silu(0.5 * terms[p][i]) for p in range(2)) for i in range(2)]


def joined(mixed, sums, main, which):
    def at(p, a, n):
        return [x + y for x, y in zip(unpack(mixed[p, a : a + n], main, which), split(sums[p, a : a + n], main))]

    return at


def far_kernel(
    main, flags, got, own, up, down, start, end, first, tails_first, second, tails_second, r_far, taps, mixed,
    out, here, total, spread, edge_h, r, sums,
):
    half = got.shape[0]
    cols = 2 * half
    count, size = half // 2, cols * SUB
    step = size + PAD
    rows = step + (count + count % 2) * SUB

    def at(ref):
        return lambda k, g: [v[0] for v in split(ref[k * count + g : k * count + g + 1].astype(F32), main)]

    nearby = edge_stencil(flags, lambda g: at(own)(0, g), at(up), at(down), count, main, here, step)
    weave(inner_stencil(got_columns(got, main), lambda g: nearby[g], cols, count, here))
    weave(convolve(here, first, tails_first, total, 0, rows, main))
    spread_halves(total, spread, cols, count, main, 0, step)
    toward = [flags[TAP_FAR], flags[TAP_NEAR]]
    totals = second_convolution(
        flags, spread, (start, end), cols, count, main, second, tails_second, edge_h, here, total
    )

    residual(got_columns(got, main), totals, cols, main, r, flags[HAS_FAR] > 0)

    for p in range(2):
        sums[p] = mix([(r, toward[p])], taps, main, p)

    piece = CHUNK * SUB
    for s in range(0, size, piece):
        value = blend(r_far, joined(mixed, sums, main, 0), s, piece, main)
        store(out, s // SUB, [v.reshape(CHUNK, SUB, v.shape[-1]) for v in value])


def last_kernel(main, parts, flags, got, mixed, r_near, taps, done, out, staged, sums, sems):
    cols = done.shape[0]
    copies = [pltpu.make_async_copy(done, out.at[flags[FAR]], sems.at[parts])]
    copies[0].start()
    toward = [flags[TAP_NEAR], flags[TAP_FAR]]
    piece, halves = CHUNK * SUB, 2
    for i in range(parts):
        first, last = i * cols // parts, (i + 1) * cols // parts
        if i % (parts // halves) == 0:
            rows = slice(first * SUB, (first + cols // halves) * SUB)
            for p in range(2):
                sums[p, rows] = mix([(got, toward[p])], taps, main, p, rows)
        for c in range(first, last, CHUNK):
            value = blend(r_near, joined(mixed, sums, main, 1), c * SUB, piece, main)
            store(staged, c, [v.reshape(CHUNK, SUB, v.shape[-1]) for v in value])

        copy = pltpu.make_async_copy(
            staged.at[first:last], out.at[flags[NEAR], first:last], sems.at[i]
        )
        copy.start()
        copies.append(copy)
    for copy in copies:
        copy.wait()


VMEM = pl.BlockSpec(memory_space=pltpu.VMEM)
SMEM = pl.BlockSpec(memory_space=pltpu.SMEM)
HBM = pl.BlockSpec(memory_space=pltpu.HBM)


def call(kernel, outs, args, scratch=(), name=None, flops=0, out_specs=None, limit=24):
    return pl.pallas_call(
        kernel,
        out_shape=outs,
        in_specs=[SMEM if a.dtype == jnp.int32 else VMEM for a in args],
        out_specs=out_specs or jax.tree.map(lambda _: VMEM, outs),
        scratch_shapes=list(scratch),
        name=name,
        cost_estimate=pl.CostEstimate(flops=flops, bytes_accessed=1 << 20, transcendentals=0),
        compiler_params=pltpu.CompilerParams(vmem_limit_bytes=limit << 20),
    )(*args)


def pairs(count, start):
    links = [(i, i + 1) for i in range(start, count - 1, 2)]
    return links + [(b, a) for a, b in links]


def row_neighbours(edge):
    count = lax.axis_size("row")
    if count == 1:
        return edge, edge
    first = lax.ppermute(edge, "row", pairs(count, 0))
    if count == 2:
        return first, first
    second = lax.ppermute(edge, "row", pairs(count, 1))
    even = lax.axis_index("row") % 2 == 0
    return jnp.where(even, second, first), jnp.where(even, first, second)


def shards(latents, conv_first, conv_second, conv_time, cond_start, cond_end):
    _, rows, cols, channels = latents.shape
    main = channels // LANES * LANES
    assert latents.shape[0] == 2 and rows == SUB and 2 * (channels - main) == LANES and cols % 4 == 0
    pixels, count = rows * cols, cols // 4
    step = pixels + PAD
    width = 3 * main + 2 * LANES
    wide = 2 * main + 2 * LANES
    packed = 2 * main + LANES
    frames_n, rows_n = lax.axis_size("frame"), lax.axis_size("row")
    frame, row = lax.axis_index("frame"), lax.axis_index("row")
    odd = frame % 2
    has_far = jnp.where(odd == 1, frame < frames_n - 1, frame > 0)
    flags = jnp.stack([1 - odd, odd, 2 * odd, 2 - 2 * odd, has_far, row > 0, row < rows_n - 1]).astype(jnp.int32)
    video = jnp.transpose(latents, (0, 2, 1, 3))
    unit = 32 * pixels * LANES * LANES

    def struct(*shape, dtype=BF16):
        return jax.ShapeDtypeStruct(shape, dtype)

    here = (2 * step + PAD, width)
    work = [
        pltpu.VMEM(here, BF16), pltpu.VMEM((2 * step, wide), F32),
        pltpu.VMEM((cols + count, SUB, main + LANES), F32), pltpu.VMEM((2, count, SUB, main + LANES), F32),
    ]
    video, edge, sent = call(
        functools.partial(prepare_kernel, main),
        (struct(2, cols, SUB, main + LANES), struct(4 * count, SUB, main + LANES), struct(cols // 2, SUB, packed)),
        (flags, video), name="prepare", flops=8 * unit,
    )
    up, down = row_neighbours(edge)
    got_far = lax.ppermute(sent, "frame", pairs(frames_n, 1))
    first, second, taps = conv_first, conv_second, conv_time
    r_near, tails_first, tails_second = call(
        functools.partial(near_kernel, main),
        (struct(pixels, packed), struct(width, 2 * LANES), struct(width, 2 * LANES)),
        (flags, video, edge, up, down, cond_start, cond_end, first, second), work, "near", 24 * unit,
    )
    got_near = lax.ppermute(r_near, "frame", pairs(frames_n, 0))
    total_far = call(
        functools.partial(other_kernel, main), struct(2 * step, wide, dtype=F32),
        (flags, video, edge, up, down, cond_start, cond_end, first, tails_first, second, tails_second),
        [work[0], *work[2:]], "other", 12 * unit,
    )
    got_far, total_far = lax.optimization_barrier((got_far, total_far))
    far_edge = call(functools.partial(relay_kernel, main), struct(2 * count, SUB, main + LANES), (got_far,), name="relay")
    far_up, far_down = row_neighbours(far_edge)
    r_far, mixed = call(
        functools.partial(mix_kernel, main), (struct(pixels, packed), struct(2, pixels, packed, dtype=F32)),
        (flags, video, total_far, r_near, taps),
        name="mix", flops=2 * unit,
    )
    done = call(
        functools.partial(far_kernel, main), struct(cols, SUB, channels),
        (
            flags, got_far, far_edge, far_up, far_down, cond_start, cond_end, first, tails_first, second, tails_second,
            r_far, taps, mixed,
        ),
        [*work, pltpu.VMEM((pixels, packed), BF16), pltpu.VMEM((2, pixels, channels), F32)], "far", 12 * unit,
    )
    parts = 6
    out = call(
        functools.partial(last_kernel, main, parts), struct(2, cols, SUB, channels),
        (flags, got_near, mixed, r_near, taps, done),
        [
            pltpu.VMEM((cols, SUB, channels), BF16), pltpu.VMEM((2, pixels, channels), F32),
            pltpu.SemaphoreType.DMA((parts + 1,)),
        ],
        "last", 4 * unit, HBM,
    )
    return jnp.transpose(out, (0, 2, 1, 3))


def solution(mesh):
    placed = (P("frame", "row", None, None), P(), P(), P(), P(), P())
    return jax.shard_map(
        shards, mesh=mesh, in_specs=placed, out_specs=P("frame", "row", None, None), check_vma=False
    )
```
